512 devices in a mesh: rows: 8 (over z), cx: 8 (over y), cy: 8 (over x, core).
Axes of the slice: x: 4, y: 8, z: 8, core: 2. Of those that a mesh axis runs over, the one named last changes fastest.
Arguments:
- rows_data: float32 [32768, 1024], P(('rows', 'cx', 'cy')), may hold values from -6 to 6
- owner_rows: int32 [32768, 1], P(('rows', 'cx', 'cy')), may hold values from 0 to 63; in each aligned block of 64 rows (0 to 63, 64 to 127, ...) at most 2 rows name the same one
- slot_rows: int32 [32768], P(('rows', 'cx', 'cy')), may hold values from 0 to 2047
- centroids: float32 [131072, 1024], P(('cx', 'cy'), 'rows'), may hold values from -6 to 6
- counts: float32 [131072], P(('cx', 'cy')), may hold values from 1 to 100
- owner_cent: int32 [131072, 1], P(('cx', 'cy')), may hold values from 0 to 63; in each aligned block of 2048 rows (0 to 2047, 2048 to 4095, ...) at most 64 rows name the same one
- slot_cent: int32 [131072], P(('cx', 'cy')), may hold values from 0 to 63
- upper: float32 [4096, 1024], P(('cx', 'cy'), 'rows'), may hold values from -6 to 6
- upper_counts: float32 [4096], P(('cx', 'cy')), may hold values from 1 to 100
Outputs:
- moved: float32 [131072, 1024], P(('cx', 'cy'), 'rows')
- new_counts: float32 [131072], P(('cx', 'cy'))
- new_upper: float32 [4096, 1024], P(('cx', 'cy'), 'rows')
- new_upper_counts: float32 [4096], P(('cx', 'cy'))
The draws below stay inside these ranges and needn't reach their ends.
Inputs may be any that keep to these rules, and one draw needn't show every extreme that they name: `owner_rows`: the rows of one device name each value at most 2 times, and some device reaches it. `owner_cent`: the 2048 level-1 centroids of one shard name each value at most 64 times, and some shard reaches it.
All inputs are finite; a program needn't handle non-finite values.
Results may differ from the reference program's by a relative error of at most 0.00002.
Values sent between devices are 32-bit elements; how exact they have to be, the bound alone decides.
No kernel may reach another device: no remote copies, remote signals or barrier semaphores. Data moves between devices by JAX's collectives and lax.ppermute only.
A program may use at most 64 MiB of HBM per device.

```python
import math
import jax
import jax.numpy as jnp
import numpy as np

D = 1024
C1_DEV = 2048
K2 = 4096
TOK_DEV = 64
SHARDS = 64
C1 = 131072
K2_DEV = 64
ROWS_ALL = 32768
CAP1 = 2
CAP2 = 64


def plant(entries, rng, smallest, top_value):
    spot = [jax.random.randint(jax.random.fold_in(rng, axis), (), 0, length) for axis, length in enumerate(entries.shape)]
    main_axis = entries.shape.index(max(entries.shape))
    beside = spot[:main_axis] + [(spot[main_axis] + 1) % entries.shape[main_axis]] + spot[main_axis + 1:]
    return entries.at[tuple(spot)].set(smallest).at[tuple(beside)].set(top_value)


def block_levels(key, extent, split, least, high):
    gain, own = 1.0, jax.random.fold_in(key, 6)
    for dim, blocks in split:
        heights = jnp.exp(jax.random.uniform(jax.random.fold_in(own, dim), (blocks,), jnp.float32, least / len(split), high / len(split)))
        gain = gain * jnp.repeat(heights, extent[dim] // blocks).reshape([-1 if axis == dim else 1 for axis in range(len(extent))])
    return gain


def shared_out(key, own, number, rows, amount, top, limit, slope):
    ranking = jax.random.permutation(key, amount)
    heavy_load, ordinary = shares(amount, rows * top, limit, slope, True), shares(amount, rows * top, limit, slope, False)
    places = jnp.arange(amount)

    def named(lengths, offset_by):
        used = int((lengths > 0).sum())
        fixed = max(1, used // 4)
        passed = fixed + (places - fixed + offset_by * (used - fixed)) % max(1, amount - fixed)
        return jnp.zeros((amount,), jnp.int32).at[ranking[jnp.where(places < fixed, places, passed)]].set(jnp.asarray(lengths, jnp.int32))

    lengths = jnp.where(number % 4 == 0, named(heavy_load, number // 4), named(ordinary, number - number // 4 - 1))
    mixed = jax.random.permutation(jax.random.fold_in(own, 3), amount)
    giver, receiver = mixed[0:amount // 2 * 2:2], mixed[1:amount // 2 * 2:2]
    room = jnp.minimum(lengths[giver] - 1, limit - lengths[receiver]) // 2
    room = jnp.where((giver == ranking[0]) | (receiver == ranking[0]) | (lengths[receiver] == 0), 0, jnp.maximum(room, 0))
    passed = jax.random.randint(jax.random.fold_in(own, 4), (amount // 2,), 0, 1 << 20) % (room + 1)
    lengths = lengths.at[giver].add(-passed).at[receiver].add(passed)
    members = jnp.searchsorted(jnp.cumsum(lengths), jnp.arange(rows * top), side="right").astype(jnp.int32)
    listing = members.reshape(top, rows).T
    listing = listing[jax.random.permutation(jax.random.fold_in(own, 1), rows)]
    offset_by = jax.random.randint(jax.random.fold_in(own, 2), (rows, 1), 0, top)
    return jnp.take_along_axis(listing, (jnp.arange(top)[None, :] + offset_by) % top, axis=1)


def shares(count, total, bound, slope, full):
    weights = [(1 << 20) // math.isqrt(standing ** slope) + 1 for standing in range(1, count + 1)]
    largest = bound if full else min(bound, max(-(-total // count), total * weights[0] // sum(weights)))
    least = 1 if total - largest >= count - 1 else 0
    given, rest = [largest] + [least] * (count - 1), total - largest - least * (count - 1)
    while rest > 0:
        free = [i for i in range(1, count) if given[i] < largest] or [i for i in range(1, count) if given[i] < bound]
        mass, left = sum([weights[i] for i in free]), rest
        for i in free:
            extra = min(bound - given[i], max(1, left * weights[i] // mass), rest)
            given[i] = given[i] + extra
            rest = rest - extra
    return np.array(given)


def centred(stream_key, dims, deviation, reach, pieces=(), dtype=jnp.bfloat16):
    entries = jax.random.normal(stream_key, dims, jnp.float32) * deviation
    if len(pieces) > 0:
        entries = block_levels(stream_key, dims, pieces, -0.22, 0.18) * entries
    return jnp.clip(entries, min=-reach, max=reach).astype(dtype)


def setup_inputs(seed: int = 0) -> dict:
    arg_keys = jax.random.split(jax.random.key(seed), 10)
    rows_data = centred(arg_keys[0], (ROWS_ALL, D), 1.0, 6.0, ((0, 512),), jnp.float32)
    owner_rows_keys = jax.random.split(jax.random.fold_in(arg_keys[1], 1), ROWS_ALL // TOK_DEV)
    owner_rows_turns = jax.random.permutation(jax.random.fold_in(arg_keys[1], 3), ROWS_ALL // TOK_DEV)
    owner_rows = jax.vmap(lambda own, number: shared_out(jax.random.fold_in(arg_keys[1], 2), own, number, TOK_DEV, SHARDS, 1, CAP1, 2))(owner_rows_keys, owner_rows_turns).reshape((ROWS_ALL, 1))
    slot_rows = plant(jax.random.randint(arg_keys[2], (ROWS_ALL,), 0, C1_DEV), jax.random.fold_in(arg_keys[2], 1), 0, C1_DEV - 1).astype(jnp.int32)
    centroids = centred(arg_keys[3], (C1, D), 1.0, 6.0, ((0, 64), (1, 8)), jnp.float32)
    counts = jnp.clip(jnp.exp(math.log(100.0) - 4.6051702 * jax.random.uniform(arg_keys[4], (C1,), jnp.float32) ** block_levels(arg_keys[4], (C1,), ((0, 64),), -0.2, 0.2)), 1.0, 100.0)
    owner_cent_keys = jax.random.split(jax.random.fold_in(arg_keys[5], 1), C1 // C1_DEV)
    owner_cent_turns = jax.random.permutation(jax.random.fold_in(arg_keys[5], 3), C1 // C1_DEV)
    owner_cent = jax.vmap(lambda own, number: shared_out(jax.random.fold_in(arg_keys[5], 2), own, number, C1_DEV, SHARDS, 1, CAP2, 2))(owner_cent_keys, owner_cent_turns).reshape((C1, 1))
    slot_cent = plant(jax.random.randint(arg_keys[6], (C1,), 0, K2_DEV), jax.random.fold_in(arg_keys[6], 1), 0, K2_DEV - 1).astype(jnp.int32)
    upper = centred(arg_keys[7], (K2, D), 1.0, 6.0, ((0, 64), (1, 8)), jnp.float32)
    upper_counts = jnp.clip(jnp.exp(math.log(100.0) - 4.6051702 * jax.random.uniform(arg_keys[8], (K2,), jnp.float32) ** block_levels(arg_keys[8], (K2,), ((0, 64),), -0.2, 0.2)), 1.0, 100.0)
    return dict(rows_data=rows_data, owner_rows=owner_rows, slot_rows=slot_rows, centroids=centroids, counts=counts, owner_cent=owner_cent, slot_cent=slot_cent, upper=upper, upper_counts=upper_counts)


def reference(rows_data, owner_rows, slot_rows, centroids, counts, owner_cent, slot_cent, upper, upper_counts):
    lower_ids = owner_rows[:, 0] * C1_DEV + slot_rows
    summed = jax.ops.segment_sum(rows_data, lower_ids, num_segments=C1)
    member_counts = jax.ops.segment_sum(jnp.ones(lower_ids.shape, jnp.float32), lower_ids, num_segments=C1)
    new_counts = counts + member_counts
    moved = centroids + (summed - member_counts[:, None] * centroids) / new_counts[:, None]
    upper_ids = owner_cent[:, 0] * K2_DEV + slot_cent
    upper_summed = jax.ops.segment_sum(moved, upper_ids, num_segments=K2)
    upper_members = jax.ops.segment_sum(jnp.ones(upper_ids.shape, jnp.float32), upper_ids, num_segments=K2)
    new_upper_counts = upper_counts + upper_members
    new_upper = upper + (upper_summed - upper_members[:, None] * upper) / new_upper_counts[:, None]
    return moved, new_counts, new_upper, new_upper_counts
```

```python
import functools

import jax
import jax.numpy as jnp
from jax import lax
from jax.experimental import pallas as pl
from jax.experimental.pallas import tpu as pltpu
from jax.sharding import Mesh, PartitionSpec as P

F32 = jnp.float32
BF16 = jnp.bfloat16
LANES = 128
BLOCK = 256


def iota(shape, dim):
    return lax.broadcasted_iota(jnp.int32, shape, dim)


def onehot(mask):
    return jnp.where(mask, 1.0, 0.0).astype(BF16)


def matmul(a, b):
    return lax.dot_general(a, b, (((1,), (0,)), ((), ())), preferred_element_type=F32)


def halves(x):
    high = x.astype(BF16)
    return high, (x - high.astype(F32)).astype(BF16)


def pack_kernel(empty, rows_ref, owner_ref, slot_ref, oc_ref, sc_ref, out_ref):
    batch, width = rows_ref.shape
    shards = batch
    groups = width // LANES
    lane = iota((shards, batch), 1)
    named = owner_ref[...] == iota((shards, batch), 0)
    first = jnp.min(jnp.where(named, lane.astype(F32), float(batch)), axis=1, keepdims=True)
    sel0 = lane.astype(F32) == first
    sel1 = jnp.logical_and(named, jnp.logical_not(sel0))
    slot = slot_ref[...].astype(F32)

    def label(sel):
        one = jnp.sum(jnp.where(sel, 1.0, 0.0), axis=1, keepdims=True)
        at = jnp.sum(jnp.where(sel, slot, 0.0), axis=1, keepdims=True)
        return at + (1.0 - one) * empty

    sel = jnp.concatenate([onehot(sel0), onehot(sel1)], axis=0)
    rows = rows_ref[...]
    high = rows.astype(BF16)
    rest = rows - high.astype(F32)
    mid, low = halves(rest)
    got = matmul(sel, high) + matmul(sel, mid) + matmul(sel, low)
    members = oc_ref.shape[1]
    a = onehot(oc_ref[...] == iota((shards, members), 0))
    b = onehot(sc_ref[...] + (LANES - shards) == iota((LANES, members), 0))
    hits = lax.dot_general(a, b, (((1,), (1,)), ((), ())), preferred_element_type=F32)
    where = iota((shards, LANES), 1)
    meta = jnp.where(where == 0, label(sel0), jnp.where(where == 1, label(sel1), hits))
    for z in range(groups):
        at = pl.ds(z * shards, shards)
        cols = slice(z * LANES, (z + 1) * LANES)
        out_ref[at, 0:LANES] = got[:shards, cols]
        out_ref[at, LANES : 2 * LANES] = got[shards:, cols]
        out_ref[at, 2 * LANES : 3 * LANES] = meta


def partial_sums(ids, parts_ref, out_ref):
    rows, members = out_ref.shape[0], parts_ref.shape[0]

    def step(i, carry):
        at = pl.multiple_of(i * BLOCK, BLOCK)
        hot = onehot(ids - at == iota((BLOCK, members), 0))
        both = matmul(hot, parts_ref[...])
        out_ref[pl.ds(at, BLOCK), :] = both[:, :LANES] + both[:, LANES:]
        return carry

    lax.fori_loop(0, rows // BLOCK, step, 0, unroll=2)


def ids_of(oc_ref, sc_ref, core, width):
    owner = oc_ref[...]
    ids = lax.shift_right_logical(owner, 1) * width + sc_ref[...]
    return jnp.where(jnp.bitwise_and(owner, 1) == core, ids, -1)


def move_kernel(
    width, core_ref, got_ref, cent_ref, counts_ref, oc_ref, sc_ref,
    moved_ref, new_counts_ref, send_ref, parts_ref, hits_ref,
):
    sources = got_ref.shape[0]
    lower = cent_ref.shape[0]
    meta = got_ref[:, 2 * LANES : 3 * LANES]
    hits_ref[...] = jnp.sum(meta[:width], axis=0, keepdims=True)
    across = meta.T
    labels = jnp.concatenate([across[0:1, :], across[1:2, :]], axis=1).astype(jnp.int32)
    rows = jnp.concatenate([got_ref[:, 0:LANES], got_ref[:, LANES : 2 * LANES]], axis=0)
    high, low = halves(rows)
    rhs = jnp.concatenate([high, low, jnp.ones((2 * sources, LANES), BF16)], axis=1)
    eye = iota((LANES, LANES), 0) == iota((LANES, LANES), 1)
    for i in range(lower // BLOCK):
        at = i * BLOCK
        hot = onehot(labels - at == iota((BLOCK, 2 * sources), 0))
        both = matmul(hot, rhs)
        summed = both[:, :LANES] + both[:, LANES : 2 * LANES]
        members = both[:, 2 * LANES :]
        old = cent_ref[at : at + BLOCK, :]
        total = counts_ref[at : at + BLOCK, :] + members
        moved = old + (summed - members * old) / total
        moved_ref[at : at + BLOCK, :] = moved
        high_m, low_m = halves(moved)
        parts_ref[at : at + BLOCK, :LANES] = high_m
        parts_ref[at : at + BLOCK, LANES:] = low_m
        for j in range(BLOCK // LANES):
            block = jnp.where(eye, total[j * LANES : (j + 1) * LANES], 0.0)
            row = i * (BLOCK // LANES) + j
            new_counts_ref[row : row + 1, :] = jnp.sum(block, axis=0, keepdims=True)
    partial_sums(ids_of(oc_ref, sc_ref, 1 - core_ref[0], width), parts_ref, send_ref)


def keep_kernel(width, core_ref, parts_ref, oc_ref, sc_ref, keep_ref):
    partial_sums(ids_of(oc_ref, sc_ref, core_ref[0], width), parts_ref, keep_ref)


VMEM = pl.BlockSpec(memory_space=pltpu.VMEM)
SMEM = pl.BlockSpec(memory_space=pltpu.SMEM)
PARAMS = pltpu.CompilerParams(vmem_limit_bytes=40 * 1024 * 1024)


def call(kernel, ins, outs, flops, nbytes, name):
    return pl.pallas_call(
        kernel,
        in_specs=ins,
        out_specs=[VMEM] * len(outs),
        out_shape=[jax.ShapeDtypeStruct(s, d) for s, d in outs],
        compiler_params=PARAMS,
        cost_estimate=pl.CostEstimate(flops=flops, bytes_accessed=nbytes, transcendentals=0),
        name=name,
    )


def body(rows_data, owner_rows, slot_rows, centroids, counts, owner_cent, slot_cent, upper, upper_counts):
    everyone = ("rows", "cx", "x", "core")
    groups = lax.axis_size("rows")
    shards = lax.axis_size(("cx", "x", "core"))
    batch = rows_data.shape[0]
    lower = centroids.shape[0]
    width = upper.shape[0]
    core = lax.axis_index("core").astype(jnp.int32).reshape(1)
    oc = owner_cent.reshape(1, lower)
    sc = slot_cent.reshape(1, lower)
    sent = 3 * LANES
    (packed,) = call(
        functools.partial(pack_kernel, lower),
        [VMEM] * 5,
        [((groups * shards, sent), F32)],
        10**8, 10**6, "pack",
    )(rows_data, owner_rows.reshape(1, batch), slot_rows.reshape(1, batch), oc, sc)
    got = lax.all_to_all(packed, everyone, 0, 0, tiled=True)
    wide_counts = jnp.broadcast_to(counts[:, None], (lower, LANES))
    half = width * shards // 2
    moved, new_counts, send, parts, hits = call(
        functools.partial(move_kernel, width),
        [SMEM] + [VMEM] * 5,
        [((lower, LANES), F32), ((lower // LANES, LANES), F32), ((half, LANES), F32), ((lower, 2 * LANES), BF16), ((1, LANES), F32)],
        4 * 10**9, 4 * 10**6, "move",
    )(core, got, centroids, wide_counts, oc, sc)
    arrived = lax.ppermute(send, "core", [(0, 1), (1, 0)])
    (keep,) = call(
        functools.partial(keep_kernel, width),
        [SMEM] + [VMEM] * 3,
        [((half, LANES), F32)],
        2 * 10**9, 2 * 10**6, "keep",
    )(core, parts, oc, sc)
    pair = (keep + arrived).reshape(shards // 2, width, LANES)
    pieces = lax.all_to_all(pair, ("cx", "x"), 0, 0, tiled=True)
    upper_summed = jnp.sum(pieces, axis=0)
    upper_members = hits[0, LANES - width :]
    new_upper_counts = upper_counts + upper_members
    new_upper = upper + (upper_summed - upper_members[:, None] * upper) / new_upper_counts[:, None]
    return moved, new_counts.reshape(lower), new_upper, new_upper_counts


def solution(mesh):
    groups, outer, inner = mesh.devices.shape
    fine = Mesh(mesh.devices.reshape(groups, outer, inner // 2, 2), ("rows", "cx", "x", "core"))
    everyone = ("rows", "cx", "x", "core")
    plane = ("cx", "x", "core")
    return jax.shard_map(
        body,
        mesh=fine,
        in_specs=(
            P(everyone, None), P(everyone, None), P(everyone),
            P(plane, "rows"), P(plane), P(plane, None), P(plane),
            P(plane, "rows"), P(plane),
        ),
        out_specs=(P(plane, "rows"), P(plane), P(plane, "rows"), P(plane)),
        check_vma=False,
    )
```

```python
import functools

import jax
import jax.numpy as jnp
from jax import lax
from jax.experimental import pallas as pl
from jax.experimental.pallas import tpu as pltpu
from jax.sharding import Mesh, PartitionSpec as P

F32 = jnp.float32
BF16 = jnp.bfloat16
LANES = 128
BLOCK = 256
PARTS = 3


def iota(shape, dim):
    return lax.broadcasted_iota(jnp.int32, shape, dim)


def onehot(mask):
    return jnp.where(mask, 1.0, 0.0).astype(BF16)


def matmul(a, b):
    return lax.dot_general(a, b, (((1,), (0,)), ((), ())), preferred_element_type=F32)


def halves(x):
    high = x.astype(BF16)
    return high, (x - high.astype(F32)).astype(BF16)


def columns(row):
    return jnp.broadcast_to(row, (LANES, LANES)).T


def pack_kernel(
    empty, rows_hbm, owner_hbm, slot_hbm, oc_hbm, sc_hbm, out_ref,
    rows_ref, owner_ref, slot_ref, oc_ref, sc_ref, sems,
):
    pairs = [
        (owner_hbm, owner_ref), (slot_hbm, slot_ref), (oc_hbm, oc_ref), (sc_hbm, sc_ref), (rows_hbm, rows_ref),
    ]
    copies = [pltpu.make_async_copy(src, dst, sems.at[i]) for i, (src, dst) in enumerate(pairs)]
    for copy in copies:
        copy.start()
    for copy in copies[:4]:
        copy.wait()
    batch, width = rows_ref.shape
    shards = batch
    groups = width // LANES
    lane = iota((shards, batch), 1)
    named = owner_ref[...] == iota((shards, batch), 0)
    first = jnp.min(jnp.where(named, lane.astype(F32), float(batch)), axis=1, keepdims=True)
    sel0 = lane.astype(F32) == first
    sel1 = jnp.logical_and(named, jnp.logical_not(sel0))
    slot = slot_ref[...].astype(F32)

    def label(sel):
        return jnp.sum(jnp.where(sel, slot - empty, 0.0), axis=1, keepdims=True) + empty

    members = oc_ref.shape[1]
    a = onehot(oc_ref[...] == iota((shards, members), 0))
    b = onehot(sc_ref[...] + (LANES - shards) == iota((LANES, members), 0))
    hits = lax.dot_general(a, b, (((1,), (1,)), ((), ())), preferred_element_type=F32)
    where = iota((shards, LANES), 1)
    meta = jnp.where(where == 0, label(sel0), jnp.where(where == 1, label(sel1), hits))
    for z in range(groups):
        out_ref[pl.ds(z * shards * PARTS + 2, shards, stride=PARTS), :] = meta
    sel = jnp.concatenate([onehot(sel0), onehot(sel1)], axis=0)
    copies[4].wait()
    rows = rows_ref[...]
    high = rows.astype(BF16)
    mid, low = halves(rows - high.astype(F32))
    got = matmul(sel, high) + matmul(sel, mid) + matmul(sel, low)
    for z in range(groups):
        cols = slice(z * LANES, (z + 1) * LANES)
        for p in range(2):
            at = pl.ds(z * shards * PARTS + p, shards, stride=PARTS)
            out_ref[at, :] = got[p * shards : (p + 1) * shards, cols]


def side_kernel(counts_ref, upper_counts_ref, wide_ref, wide_upper_ref):
    for i in range(counts_ref.shape[0]):
        wide_ref[i * LANES : (i + 1) * LANES, :] = columns(counts_ref[i : i + 1, :])
    upper = upper_counts_ref[...]
    width = upper.shape[1]
    wide_upper_ref[...] = columns(jnp.concatenate([upper, jnp.zeros((1, LANES - width), F32)], axis=1))[:width]


def partial_sums(ids, parts_ref, out_ref):
    rows, members = out_ref.shape[0], parts_ref.shape[0]
    for at in range(0, rows, BLOCK):
        hot = onehot(ids - at == iota((BLOCK, members), 0))
        both = matmul(hot, parts_ref[...])
        out_ref[at : at + BLOCK, :] = both[:, :LANES] + both[:, LANES:]


def ids_of(oc_ref, sc_ref, core, width):
    owner = oc_ref[...]
    ids = lax.shift_right_logical(owner, 1) * width + sc_ref[...]
    return jnp.where(jnp.bitwise_and(owner, 1) == core, ids, -1)


def move_kernel(
    width, core_ref, got_ref, cent_ref, counts_ref, oc_ref, sc_ref,
    moved_hbm, new_counts_ref, send_ref, parts_ref, hits_ref, moved_ref, sem,
):
    sources = got_ref.shape[0] // PARTS
    lower = cent_ref.shape[0]
    part = [got_ref[pl.ds(i, sources, stride=PARTS), :] for i in range(PARTS)]
    meta = part[2]
    hits_ref[...] = jnp.sum(meta[:width], axis=0, keepdims=True)
    across = meta.T
    labels = jnp.concatenate([across[0:1, :], across[1:2, :]], axis=1).astype(jnp.int32)
    rows = jnp.concatenate(part[:2], axis=0)
    high, low = halves(rows)
    rhs = jnp.concatenate([high, low, jnp.ones((2 * sources, LANES), BF16)], axis=1)
    eye = iota((LANES, LANES), 0) == iota((LANES, LANES), 1)
    for i in range(lower // BLOCK):
        at = i * BLOCK
        hot = onehot(labels - at == iota((BLOCK, 2 * sources), 0))
        both = matmul(hot, rhs)
        summed = both[:, :LANES] + both[:, LANES : 2 * LANES]
        members = both[:, 2 * LANES :]
        old = cent_ref[at : at + BLOCK, :]
        total = counts_ref[at : at + BLOCK, :] + members
        moved = old + (summed - members * old) / total
        moved_ref[at : at + BLOCK, :] = moved
        high_m, low_m = halves(moved)
        parts_ref[at : at + BLOCK, :LANES] = high_m
        parts_ref[at : at + BLOCK, LANES:] = low_m
        for j in range(BLOCK // LANES):
            block = jnp.where(eye, total[j * LANES : (j + 1) * LANES], 0.0)
            row = i * (BLOCK // LANES) + j
            new_counts_ref[row : row + 1, :] = jnp.sum(block, axis=0, keepdims=True)
    copy = pltpu.make_async_copy(moved_ref, moved_hbm, sem)
    copy.start()
    partial_sums(ids_of(oc_ref, sc_ref, 1 - core_ref[0], width), parts_ref, send_ref)
    copy.wait()


def keep_kernel(
    width, core_ref, parts_ref, oc_ref, sc_ref, hits_ref, upper_counts_ref, keep_ref, members_ref, new_counts_ref,
):
    hits = hits_ref[...]
    members_ref[...] = columns(hits)[LANES - width :]
    new_counts_ref[...] = upper_counts_ref[...] + hits[:, LANES - width :]
    partial_sums(ids_of(oc_ref, sc_ref, core_ref[0], width), parts_ref, keep_ref)


def finish_kernel(pieces_ref, upper_ref, members_ref, counts_ref, out_ref):
    summed = jnp.sum(pieces_ref[...], axis=0)
    old, members = upper_ref[...], members_ref[...]
    out_ref[...] = old + (summed - members * old) / (counts_ref[...] + members)


VMEM = pl.BlockSpec(memory_space=pltpu.VMEM)
ANY = pl.BlockSpec(memory_space=pl.ANY)
SMEM = pl.BlockSpec(memory_space=pltpu.SMEM)


def call(kernel, ins, outs, flops, nbytes, name, out_specs=None, scratch=(), vmem=40):
    return pl.pallas_call(
        kernel,
        in_specs=ins,
        out_specs=out_specs or [VMEM] * len(outs),
        out_shape=[jax.ShapeDtypeStruct(s, d) for s, d in outs],
        scratch_shapes=list(scratch),
        compiler_params=pltpu.CompilerParams(vmem_limit_bytes=vmem * 1024 * 1024),
        cost_estimate=pl.CostEstimate(flops=flops, bytes_accessed=nbytes, transcendentals=0),
        name=name,
    )


def body(rows_data, owner_rows, slot_rows, centroids, counts, owner_cent, slot_cent, upper, upper_counts):
    everyone = ("rows", "cx", "x", "core")
    groups = lax.axis_size("rows")
    shards = lax.axis_size(("cx", "x", "core"))
    pairs = shards // 2
    devices = groups * shards
    batch, features = rows_data.shape
    lower = centroids.shape[0]
    width = upper.shape[0]
    core = lax.axis_index("core").astype(jnp.int32).reshape(1)
    oc = owner_cent.reshape(1, lower)
    sc = slot_cent.reshape(1, lower)
    half = width * pairs
    ints = lambda n: pltpu.VMEM((1, n), jnp.int32)
    (packed,) = call(
        functools.partial(pack_kernel, float(lower)),
        [ANY] * 5,
        [((devices * PARTS, LANES), F32)],
        10**8, 10**6, "pack", None,
        [pltpu.VMEM((batch, features), F32), ints(batch), ints(batch), ints(lower), ints(lower), pltpu.SemaphoreType.DMA((5,))],
        63,
    )(rows_data, owner_rows.reshape(1, batch), slot_rows.reshape(1, batch), oc, sc)
    got = lax.all_to_all(packed.reshape(devices, 1, PARTS * LANES), everyone, 0, 0, tiled=True)
    got = got.reshape(devices * PARTS, LANES)
    wide_counts, wide_upper = call(
        side_kernel,
        [VMEM] * 2,
        [((lower, LANES), F32), ((width, LANES), F32)],
        10**7, 10**6, "side",
    )(counts.reshape(lower // LANES, LANES), upper_counts.reshape(1, width))
    moved, new_counts, send, parts, hits = call(
        functools.partial(move_kernel, width),
        [SMEM] + [VMEM] * 5,
        [((lower, LANES), F32), ((lower // LANES, LANES), F32), ((half, LANES), F32), ((lower, 2 * LANES), BF16), ((1, LANES), F32)],
        4 * 10**9, 4 * 10**6, "move", [ANY] + [VMEM] * 4,
        [pltpu.VMEM((lower, LANES), F32), pltpu.SemaphoreType.DMA],
    )(core, got, centroids, wide_counts, oc, sc)
    arrived = lax.ppermute(send, "core", [(0, 1), (1, 0)])
    keep, members, new_upper_counts = call(
        functools.partial(keep_kernel, width),
        [SMEM] + [VMEM] * 5,
        [((half, LANES), F32), ((width, LANES), F32), ((1, width), F32)],
        2 * 10**9, 2 * 10**6, "keep",
    )(core, parts, oc, sc, hits, upper_counts.reshape(1, width))
    pair = (keep + arrived).reshape(pairs, width, LANES)
    pieces = lax.all_to_all(pair, ("cx", "x"), 0, 0, tiled=True)
    (new_upper,) = call(
        finish_kernel,
        [VMEM] * 4,
        [((width, LANES), F32)],
        10**6, 10**6, "finish",
    )(pieces, upper, members, wide_upper)
    return moved, new_counts.reshape(lower), new_upper, new_upper_counts.reshape(width)


def solution(mesh):
    groups, outer, inner = mesh.devices.shape
    fine = Mesh(mesh.devices.reshape(groups, outer, inner // 2, 2), ("rows", "cx", "x", "core"))
    everyone = ("rows", "cx", "x", "core")
    plane = ("cx", "x", "core")
    return jax.shard_map(
        body,
        mesh=fine,
        in_specs=(
            P(everyone, None), P(everyone, None), P(everyone),
            P(plane, "rows"), P(plane), P(plane, None), P(plane),
            P(plane, "rows"), P(plane),
        ),
        out_specs=(P(plane, "rows"), P(plane), P(plane, "rows"), P(plane)),
        check_vma=False,
    )
```

```python
import functools

import jax
import jax.numpy as jnp
from jax import lax
from jax.experimental import pallas as pl
from jax.experimental.pallas import tpu as pltpu
from jax.sharding import Mesh, PartitionSpec as P

F32 = jnp.float32
BF16 = jnp.bfloat16
LANES = 128
BLOCK = 256
PARTS = 3


def iota(shape, dim):
    return lax.broadcasted_iota(jnp.int32, shape, dim)


def onehot(mask):
    return jnp.where(mask, 1.0, 0.0).astype(BF16)


def matmul(a, b):
    return lax.dot_general(a, b, (((1,), (0,)), ((), ())), preferred_element_type=F32)


def halves(x):
    high = x.astype(BF16)
    return high, (x - high.astype(F32)).astype(BF16)


def columns(row):
    return jnp.broadcast_to(row, (LANES, LANES)).T


def pack_kernel(
    empty, rows_hbm, owner_hbm, slot_hbm, oc_hbm, sc_hbm, out_ref,
    rows_ref, owner_ref, slot_ref, oc_ref, sc_ref, sems,
):
    moves = [
        (owner_hbm, owner_ref), (slot_hbm, slot_ref), (oc_hbm, oc_ref), (sc_hbm, sc_ref), (rows_hbm, rows_ref),
    ]
    copies = [pltpu.make_async_copy(src, dst, sems.at[i]) for i, (src, dst) in enumerate(moves)]
    for copy in copies:
        copy.start()
    for copy in copies[:4]:
        copy.wait()
    batch, width = rows_ref.shape
    shards = batch
    groups = width // LANES
    pairs = shards // 2

    def shard_at(shape):
        at = iota(shape, 0)
        return jnp.where(at < pairs, 2 * at, 2 * at - (shards - 1))

    lane = iota((shards, batch), 1)
    named = owner_ref[...] == shard_at((shards, batch))
    first = jnp.min(jnp.where(named, lane.astype(F32), float(batch)), axis=1, keepdims=True)
    sel0 = lane.astype(F32) == first
    sel1 = jnp.logical_and(named, jnp.logical_not(sel0))
    slot = slot_ref[...].astype(F32)

    def label(sel):
        return jnp.sum(jnp.where(sel, slot - empty, 0.0), axis=1, keepdims=True) + empty

    members = oc_ref.shape[1]
    a = onehot(oc_ref[...] == shard_at((shards, members)))
    b = onehot(sc_ref[...] + (LANES - shards) == iota((LANES, members), 0))
    hits = lax.dot_general(a, b, (((1,), (1,)), ((), ())), preferred_element_type=F32)
    where = iota((shards, LANES), 1)
    meta = jnp.where(where == 0, label(sel0), jnp.where(where == 1, label(sel1), hits))

    def spots(core, z, part):
        return pl.ds((core * groups + z) * pairs * PARTS + part, pairs, stride=PARTS)

    for z in range(groups):
        for core in range(2):
            out_ref[spots(core, z, 2), :] = meta[core * pairs : (core + 1) * pairs]
    sel = jnp.concatenate([onehot(sel0), onehot(sel1)], axis=0)
    copies[4].wait()
    rows = rows_ref[...]
    high = rows.astype(BF16)
    mid, low = halves(rows - high.astype(F32))
    got = matmul(sel, high) + matmul(sel, mid) + matmul(sel, low)
    for z in range(groups):
        cols = slice(z * LANES, (z + 1) * LANES)
        for p in range(2):
            for core in range(2):
                at = p * shards + core * pairs
                out_ref[spots(core, z, p), :] = got[at : at + pairs, cols]


def side_kernel(counts_ref, upper_counts_ref, wide_ref, wide_upper_ref):
    for i in range(counts_ref.shape[0]):
        wide_ref[i * LANES : (i + 1) * LANES, :] = columns(counts_ref[i : i + 1, :])
    upper = upper_counts_ref[...]
    width = upper.shape[1]
    wide_upper_ref[...] = columns(jnp.concatenate([upper, jnp.zeros((1, LANES - width), F32)], axis=1))[:width]


def partial_sums(ids, parts_ref, out_ref):
    rows, members = out_ref.shape[0], parts_ref.shape[0]
    for at in range(0, rows, BLOCK):
        hot = onehot(ids - at == iota((BLOCK, members), 0))
        both = matmul(hot, parts_ref[...])
        out_ref[at : at + BLOCK, :] = both[:, :LANES] + both[:, LANES:]


def ids_of(oc_ref, sc_ref, core, width):
    owner = oc_ref[...]
    ids = lax.shift_right_logical(owner, 1) * width + sc_ref[...]
    return jnp.where(jnp.bitwise_and(owner, 1) == core, ids, -1)


def move_kernel(
    width, pairs, core_ref, got_ref, cent_ref, counts_ref, oc_ref, sc_ref,
    moved_hbm, new_counts_ref, send_ref, parts_ref, hits_ref, moved_ref, sem,
):
    sources = got_ref.shape[0] // PARTS
    lower = cent_ref.shape[0]
    part = [got_ref[pl.ds(i, sources, stride=PARTS), :] for i in range(PARTS)]
    meta = part[2]
    half = sources // 2
    counted = meta[:pairs] + meta[half : half + pairs]
    hits_ref[...] = jnp.sum(counted, axis=0, keepdims=True)
    across = meta.T
    labels = jnp.concatenate([across[0:1, :], across[1:2, :]], axis=1).astype(jnp.int32)
    rows = jnp.concatenate(part[:2], axis=0)
    high, low = halves(rows)
    rhs = jnp.concatenate([high, low, jnp.ones((2 * sources, LANES), BF16)], axis=1)
    eye = iota((LANES, LANES), 0) == iota((LANES, LANES), 1)
    for i in range(lower // BLOCK):
        at = i * BLOCK
        hot = onehot(labels - at == iota((BLOCK, 2 * sources), 0))
        both = matmul(hot, rhs)
        summed = both[:, :LANES] + both[:, LANES : 2 * LANES]
        members = both[:, 2 * LANES :]
        old = cent_ref[at : at + BLOCK, :]
        total = counts_ref[at : at + BLOCK, :] + members
        moved = old + (summed - members * old) / total
        moved_ref[at : at + BLOCK, :] = moved
        high_m, low_m = halves(moved)
        parts_ref[at : at + BLOCK, :LANES] = high_m
        parts_ref[at : at + BLOCK, LANES:] = low_m
        for j in range(BLOCK // LANES):
            block = jnp.where(eye, total[j * LANES : (j + 1) * LANES], 0.0)
            row = i * (BLOCK // LANES) + j
            new_counts_ref[row : row + 1, :] = jnp.sum(block, axis=0, keepdims=True)
    copy = pltpu.make_async_copy(moved_ref, moved_hbm, sem)
    copy.start()
    partial_sums(ids_of(oc_ref, sc_ref, 1 - core_ref[0], width), parts_ref, send_ref)
    copy.wait()


def keep_kernel(
    width, core_ref, parts_ref, oc_ref, sc_ref, hits_ref, upper_counts_ref, keep_ref, members_ref, new_counts_ref,
):
    hits = hits_ref[...]
    members_ref[...] = columns(hits)[LANES - width :]
    new_counts_ref[...] = upper_counts_ref[...] + hits[:, LANES - width :]
    partial_sums(ids_of(oc_ref, sc_ref, core_ref[0], width), parts_ref, keep_ref)


def finish_kernel(pieces_ref, upper_ref, members_ref, counts_ref, out_ref):
    summed = jnp.sum(pieces_ref[...], axis=0)
    old, members = upper_ref[...], members_ref[...]
    out_ref[...] = old + (summed - members * old) / (counts_ref[...] + members)


VMEM = pl.BlockSpec(memory_space=pltpu.VMEM)
ANY = pl.BlockSpec(memory_space=pl.ANY)
SMEM = pl.BlockSpec(memory_space=pltpu.SMEM)


def call(kernel, ins, outs, flops, nbytes, name, out_specs=None, scratch=(), vmem=40):
    return pl.pallas_call(
        kernel,
        in_specs=ins,
        out_specs=out_specs or [VMEM] * len(outs),
        out_shape=[jax.ShapeDtypeStruct(s, d) for s, d in outs],
        scratch_shapes=list(scratch),
        compiler_params=pltpu.CompilerParams(vmem_limit_bytes=vmem * 1024 * 1024),
        cost_estimate=pl.CostEstimate(flops=flops, bytes_accessed=nbytes, transcendentals=0),
        name=name,
    )


def body(rows_data, owner_rows, slot_rows, centroids, counts, owner_cent, slot_cent, upper, upper_counts):
    exchange = ("core", "rows", "cx", "x")
    groups = lax.axis_size("rows")
    shards = lax.axis_size(("cx", "x", "core"))
    pairs = shards // 2
    devices = groups * shards
    batch, features = rows_data.shape
    lower = centroids.shape[0]
    width = upper.shape[0]
    core = lax.axis_index("core").astype(jnp.int32).reshape(1)
    oc = owner_cent.reshape(1, lower)
    sc = slot_cent.reshape(1, lower)
    half = width * pairs
    ints = lambda n: pltpu.VMEM((1, n), jnp.int32)
    (packed,) = call(
        functools.partial(pack_kernel, float(lower)),
        [ANY] * 5,
        [((devices * PARTS, LANES), F32)],
        10**8, 10**6, "pack", None,
        [pltpu.VMEM((batch, features), F32), ints(batch), ints(batch), ints(lower), ints(lower), pltpu.SemaphoreType.DMA((5,))],
        63,
    )(rows_data, owner_rows.reshape(1, batch), slot_rows.reshape(1, batch), oc, sc)
    got = lax.all_to_all(packed.reshape(devices, 1, PARTS * LANES), exchange, 0, 0, tiled=True)
    got = got.reshape(devices * PARTS, LANES)
    wide_counts, wide_upper = call(
        side_kernel,
        [VMEM] * 2,
        [((lower, LANES), F32), ((width, LANES), F32)],
        10**7, 10**6, "side",
    )(counts.reshape(lower // LANES, LANES), upper_counts.reshape(1, width))
    moved, new_counts, send, parts, hits = call(
        functools.partial(move_kernel, width, pairs),
        [SMEM] + [VMEM] * 5,
        [((lower, LANES), F32), ((lower // LANES, LANES), F32), ((half, LANES), F32), ((lower, 2 * LANES), BF16), ((1, LANES), F32)],
        4 * 10**9, 4 * 10**6, "move", [ANY] + [VMEM] * 4,
        [pltpu.VMEM((lower, LANES), F32), pltpu.SemaphoreType.DMA],
    )(core, got, centroids, wide_counts, oc, sc)
    arrived = lax.ppermute(send, "core", [(0, 1), (1, 0)])
    keep, members, new_upper_counts = call(
        functools.partial(keep_kernel, width),
        [SMEM] + [VMEM] * 5,
        [((half, LANES), F32), ((width, LANES), F32), ((1, width), F32)],
        2 * 10**9, 2 * 10**6, "keep",
    )(core, parts, oc, sc, hits, upper_counts.reshape(1, width))
    pair = (keep + arrived).reshape(pairs, width, LANES)
    pieces = lax.all_to_all(pair, ("cx", "x"), 0, 0, tiled=True)
    (new_upper,) = call(
        finish_kernel,
        [VMEM] * 4,
        [((width, LANES), F32)],
        10**6, 10**6, "finish",
    )(pieces, upper, members, wide_upper)
    return moved, new_counts.reshape(lower), new_upper, new_upper_counts.reshape(width)


def solution(mesh):
    groups, outer, inner = mesh.devices.shape
    fine = Mesh(mesh.devices.reshape(groups, outer, inner // 2, 2), ("rows", "cx", "x", "core"))
    everyone = ("rows", "cx", "x", "core")
    plane = ("cx", "x", "core")
    return jax.shard_map(
        body,
        mesh=fine,
        in_specs=(
            P(everyone, None), P(everyone, None), P(everyone),
            P(plane, "rows"), P(plane), P(plane, None), P(plane),
            P(plane, "rows"), P(plane),
        ),
        out_specs=(P(plane, "rows"), P(plane), P(plane, "rows"), P(plane)),
        check_vma=False,
    )
```

```python
import functools

import jax
import jax.numpy as jnp
from jax import lax
from jax.experimental import pallas as pl
from jax.experimental.pallas import tpu as pltpu
from jax.sharding import Mesh, PartitionSpec as P

F32 = jnp.float32
BF16 = jnp.bfloat16
LANES = 128
BLOCK = 256
PARTS = 3


def iota(shape, dim):
    return lax.broadcasted_iota(jnp.int32, shape, dim)


def onehot(mask):
    return jnp.where(mask, 1.0, 0.0).astype(BF16)


def matmul(a, b):
    return lax.dot_general(a, b, (((1,), (0,)), ((), ())), preferred_element_type=F32)


def halves(x):
    high = x.astype(BF16)
    return high, (x - high.astype(F32)).astype(BF16)


def columns(row):
    return jnp.broadcast_to(row, (LANES, LANES)).T


def pack_kernel(
    empty, rows_hbm, owner_hbm, slot_hbm, oc_hbm, sc_hbm, out_ref,
    rows_ref, owner_ref, slot_ref, oc_ref, sc_ref, sems,
):
    pairs = [
        (owner_hbm, owner_ref), (slot_hbm, slot_ref), (oc_hbm, oc_ref), (sc_hbm, sc_ref), (rows_hbm, rows_ref),
    ]
    copies = [pltpu.make_async_copy(src, dst, sems.at[i]) for i, (src, dst) in enumerate(pairs)]
    for copy in copies:
        copy.start()
    for copy in copies[:4]:
        copy.wait()
    batch, width = rows_ref.shape
    shards = batch
    groups = width // LANES
    lane = iota((shards, batch), 1)
    named = owner_ref[...] == iota((shards, batch), 0)
    first = jnp.min(jnp.where(named, lane.astype(F32), float(batch)), axis=1, keepdims=True)
    sel0 = lane.astype(F32) == first
    sel1 = jnp.logical_and(named, jnp.logical_not(sel0))
    slot = slot_ref[...].astype(F32)

    def label(sel):
        return jnp.sum(jnp.where(sel, slot - empty, 0.0), axis=1, keepdims=True) + empty

    members = oc_ref.shape[1]
    a = onehot(oc_ref[...] == iota((shards, members), 0))
    b = onehot(sc_ref[...] + (LANES - shards) == iota((LANES, members), 0))
    hits = lax.dot_general(a, b, (((1,), (1,)), ((), ())), preferred_element_type=F32)
    where = iota((shards, LANES), 1)
    meta = jnp.where(where == 0, label(sel0), jnp.where(where == 1, label(sel1), hits))
    for z in range(groups):
        out_ref[pl.ds(z * shards * PARTS + 2, shards, stride=PARTS), :] = meta
    sel = jnp.concatenate([onehot(sel0), onehot(sel1)], axis=0)
    copies[4].wait()
    rows = rows_ref[...]
    high = rows.astype(BF16)
    mid, low = halves(rows - high.astype(F32))
    got = matmul(sel, high) + matmul(sel, mid) + matmul(sel, low)
    for z in range(groups):
        cols = slice(z * LANES, (z + 1) * LANES)
        for p in range(2):
            at = pl.ds(z * shards * PARTS + p, shards, stride=PARTS)
            out_ref[at, :] = got[p * shards : (p + 1) * shards, cols]


def side_kernel(counts_ref, upper_counts_ref, wide_ref, wide_upper_ref):
    for i in range(counts_ref.shape[0]):
        wide_ref[i * LANES : (i + 1) * LANES, :] = columns(counts_ref[i : i + 1, :])
    upper = upper_counts_ref[...]
    width = upper.shape[1]
    wide_upper_ref[...] = columns(jnp.concatenate([upper, jnp.zeros((1, LANES - width), F32)], axis=1))[:width]


def partial_sums(ids, parts_ref, out_ref):
    rows, members = out_ref.shape[0], parts_ref.shape[0]
    for at in range(0, rows, BLOCK):
        hot = onehot(ids - at == iota((BLOCK, members), 0))
        both = matmul(hot, parts_ref[...])
        out_ref[at : at + BLOCK, :] = both[:, :LANES] + both[:, LANES:]


def ids_of(oc_ref, sc_ref, core, width, places):
    owner = oc_ref[...]
    outer, inner, fold = places
    x = jnp.bitwise_and(lax.shift_right_logical(owner, 1), inner - 1)
    y = owner // (2 * inner)
    low, high = jnp.bitwise_and(y, fold - 1), y // fold
    first = x * outer + y
    other = low * (inner * outer // fold) + high * inner + x
    mine = jnp.bitwise_and(owner, 1)
    ids = jnp.where(mine == 0, first, other) * width + sc_ref[...]
    return jnp.where(mine == core, ids, -1)


def move_kernel(
    width, places, core_ref, got_ref, cent_ref, counts_ref, oc_ref, sc_ref,
    moved_hbm, new_counts_ref, send_ref, parts_ref, hits_ref, moved_ref, sem,
):
    sources = got_ref.shape[0] // PARTS
    lower = cent_ref.shape[0]
    part = [got_ref[pl.ds(i, sources, stride=PARTS), :] for i in range(PARTS)]
    meta = part[2]
    hits_ref[...] = jnp.sum(meta[:width], axis=0, keepdims=True)
    across = meta.T
    labels = jnp.concatenate([across[0:1, :], across[1:2, :]], axis=1).astype(jnp.int32)
    rows = jnp.concatenate(part[:2], axis=0)
    high, low = halves(rows)
    rhs = jnp.concatenate([high, low, jnp.ones((2 * sources, LANES), BF16)], axis=1)
    eye = iota((LANES, LANES), 0) == iota((LANES, LANES), 1)
    for i in range(lower // BLOCK):
        at = i * BLOCK
        hot = onehot(labels - at == iota((BLOCK, 2 * sources), 0))
        both = matmul(hot, rhs)
        summed = both[:, :LANES] + both[:, LANES : 2 * LANES]
        members = both[:, 2 * LANES :]
        old = cent_ref[at : at + BLOCK, :]
        total = counts_ref[at : at + BLOCK, :] + members
        moved = old + (summed - members * old) / total
        moved_ref[at : at + BLOCK, :] = moved
        high_m, low_m = halves(moved)
        parts_ref[at : at + BLOCK, :LANES] = high_m
        parts_ref[at : at + BLOCK, LANES:] = low_m
        for j in range(BLOCK // LANES):
            block = jnp.where(eye, total[j * LANES : (j + 1) * LANES], 0.0)
            row = i * (BLOCK // LANES) + j
            new_counts_ref[row : row + 1, :] = jnp.sum(block, axis=0, keepdims=True)
    copy = pltpu.make_async_copy(moved_ref, moved_hbm, sem)
    copy.start()
    partial_sums(ids_of(oc_ref, sc_ref, 1 - core_ref[0], width, places), parts_ref, send_ref)
    copy.wait()


def keep_kernel(
    width, places, core_ref, parts_ref, oc_ref, sc_ref, hits_ref, upper_counts_ref, keep_ref, members_ref, new_counts_ref,
):
    hits = hits_ref[...]
    members_ref[...] = columns(hits)[LANES - width :]
    new_counts_ref[...] = upper_counts_ref[...] + hits[:, LANES - width :]
    partial_sums(ids_of(oc_ref, sc_ref, core_ref[0], width, places), parts_ref, keep_ref)


def finish_kernel(pieces_ref, upper_ref, members_ref, counts_ref, out_ref):
    summed = jnp.sum(pieces_ref[...], axis=0)
    old, members = upper_ref[...], members_ref[...]
    out_ref[...] = old + (summed - members * old) / (counts_ref[...] + members)


VMEM = pl.BlockSpec(memory_space=pltpu.VMEM)
ANY = pl.BlockSpec(memory_space=pl.ANY)
SMEM = pl.BlockSpec(memory_space=pltpu.SMEM)


def call(kernel, ins, outs, flops, nbytes, name, out_specs=None, scratch=(), vmem=40):
    return pl.pallas_call(
        kernel,
        in_specs=ins,
        out_specs=out_specs or [VMEM] * len(outs),
        out_shape=[jax.ShapeDtypeStruct(s, d) for s, d in outs],
        scratch_shapes=list(scratch),
        compiler_params=pltpu.CompilerParams(vmem_limit_bytes=vmem * 1024 * 1024),
        cost_estimate=pl.CostEstimate(flops=flops, bytes_accessed=nbytes, transcendentals=0),
        name=name,
    )


def body(places, rows_data, owner_rows, slot_rows, centroids, counts, owner_cent, slot_cent, upper, upper_counts):
    groups, shards = lax.axis_size("rows"), lax.axis_size("plane")
    pairs = shards // 2
    devices = groups * shards
    batch, features = rows_data.shape
    lower = centroids.shape[0]
    width = upper.shape[0]
    core = jnp.bitwise_and(lax.axis_index("plane"), 1).astype(jnp.int32).reshape(1)
    oc = owner_cent.reshape(1, lower)
    sc = slot_cent.reshape(1, lower)
    half = width * pairs
    ints = lambda n: pltpu.VMEM((1, n), jnp.int32)
    (packed,) = call(
        functools.partial(pack_kernel, float(lower)),
        [ANY] * 5,
        [((devices * PARTS, LANES), F32)],
        10**8, 10**6, "pack", None,
        [pltpu.VMEM((batch, features), F32), ints(batch), ints(batch), ints(lower), ints(lower), pltpu.SemaphoreType.DMA((5,))],
        63,
    )(rows_data, owner_rows.reshape(1, batch), slot_rows.reshape(1, batch), oc, sc)
    got = lax.all_to_all(packed.reshape(devices, 1, PARTS * LANES), ("rows", "plane"), 0, 0, tiled=True)
    got = got.reshape(devices * PARTS, LANES)
    wide_counts, wide_upper = call(
        side_kernel,
        [VMEM] * 2,
        [((lower, LANES), F32), ((width, LANES), F32)],
        10**7, 10**6, "side",
    )(counts.reshape(lower // LANES, LANES), upper_counts.reshape(1, width))
    moved, new_counts, send, parts, hits = call(
        functools.partial(move_kernel, width, places),
        [SMEM] + [VMEM] * 5,
        [((lower, LANES), F32), ((lower // LANES, LANES), F32), ((half, LANES), F32), ((lower, 2 * LANES), BF16), ((1, LANES), F32)],
        4 * 10**9, 4 * 10**6, "move", [ANY] + [VMEM] * 4,
        [pltpu.VMEM((lower, LANES), F32), pltpu.SemaphoreType.DMA],
    )(core, got, centroids, wide_counts, oc, sc)
    arrived = lax.ppermute(send, "plane", [(s, s ^ 1) for s in range(shards)])
    keep, members, new_upper_counts = call(
        functools.partial(keep_kernel, width, places),
        [SMEM] + [VMEM] * 5,
        [((half, LANES), F32), ((width, LANES), F32), ((1, width), F32)],
        2 * 10**9, 2 * 10**6, "keep",
    )(core, parts, oc, sc, hits, upper_counts.reshape(1, width))
    outer, inner, fold = places
    at = lambda y, x, c: (y * inner + x) * 2 + c
    near = [[at(y, x, 0) for x in range(inner)] for y in range(outer)]
    near += [[at(h * fold + l, x, 1) for l in range(fold)] for h in range(outer // fold) for x in range(inner)]
    far = [[at(y, x, 0) for y in range(outer)] for x in range(inner)]
    far += [[at(h * fold + l, x, 1) for h in range(outer // fold) for x in range(inner)] for l in range(fold)]
    pair = (keep + arrived).reshape(inner, outer * width, LANES)
    merged = jnp.sum(lax.all_to_all(pair, "plane", 0, 0, axis_index_groups=near, tiled=True), axis=0)
    merged = merged.reshape(outer, width, LANES)
    pieces = lax.all_to_all(merged, "plane", 0, 0, axis_index_groups=far, tiled=True)
    (new_upper,) = call(
        finish_kernel,
        [VMEM] * 4,
        [((width, LANES), F32)],
        10**6, 10**6, "finish",
    )(pieces, upper, members, wide_upper)
    return moved, new_counts.reshape(lower), new_upper, new_upper_counts.reshape(width)


def solution(mesh):
    groups, outer, inner = mesh.devices.shape
    fine = Mesh(mesh.devices.reshape(groups, outer * inner), ("rows", "plane"))
    everyone = ("rows", "plane")
    inner = inner // 2
    return jax.shard_map(
        functools.partial(body, (outer, inner, inner)),
        mesh=fine,
        in_specs=(
            P(everyone, None), P(everyone, None), P(everyone),
            P("plane", "rows"), P("plane"), P("plane", None), P("plane"),
            P("plane", "rows"), P("plane"),
        ),
        out_specs=(P("plane", "rows"), P("plane"), P("plane", "rows"), P("plane")),
        check_vma=False,
    )
```

```python
import functools

import jax
import jax.numpy as jnp
from jax import lax
from jax.experimental import pallas as pl
from jax.experimental.pallas import tpu as pltpu
from jax.sharding import Mesh, PartitionSpec as P

F32 = jnp.float32
BF16 = jnp.bfloat16
LANES = 128
BLOCK = 256
PARTS = 3


def iota(shape, dim):
    return lax.broadcasted_iota(jnp.int32, shape, dim)


def onehot(mask):
    return jnp.where(mask, 1.0, 0.0).astype(BF16)


def matmul(a, b):
    return lax.dot_general(a, b, (((1,), (0,)), ((), ())), preferred_element_type=F32)


def halves(x):
    high = x.astype(BF16)
    return high, (x - high.astype(F32)).astype(BF16)


def columns(row):
    return jnp.broadcast_to(row, (LANES, LANES)).T


def pack_kernel(
    empty, rows_hbm, owner_hbm, slot_hbm, oc_hbm, sc_hbm, out_ref,
    rows_ref, owner_ref, slot_ref, oc_ref, sc_ref, sems,
):
    pairs = [
        (owner_hbm, owner_ref), (slot_hbm, slot_ref), (oc_hbm, oc_ref), (sc_hbm, sc_ref), (rows_hbm, rows_ref),
    ]
    copies = [pltpu.make_async_copy(src, dst, sems.at[i]) for i, (src, dst) in enumerate(pairs)]
    for copy in copies:
        copy.start()
    for copy in copies[:4]:
        copy.wait()
    batch, width = rows_ref.shape
    shards = batch
    groups = width // LANES
    lane = iota((shards, batch), 1)
    named = owner_ref[...] == iota((shards, batch), 0)
    first = jnp.min(jnp.where(named, lane.astype(F32), float(batch)), axis=1, keepdims=True)
    sel0 = lane.astype(F32) == first
    sel1 = jnp.logical_and(named, jnp.logical_not(sel0))
    slot = slot_ref[...].astype(F32)

    def label(sel):
        return jnp.sum(jnp.where(sel, slot - empty, 0.0), axis=1, keepdims=True) + empty

    members = oc_ref.shape[1]
    a = onehot(oc_ref[...] == iota((shards, members), 0))
    b = onehot(sc_ref[...] + (LANES - shards) == iota((LANES, members), 0))
    hits = lax.dot_general(a, b, (((1,), (1,)), ((), ())), preferred_element_type=F32)
    where = iota((shards, LANES), 1)
    meta = jnp.where(where == 0, label(sel0), jnp.where(where == 1, label(sel1), hits))
    for z in range(groups):
        out_ref[pl.ds(z * shards * PARTS + 2, shards, stride=PARTS), :] = meta
    sel = jnp.concatenate([onehot(sel0), onehot(sel1)], axis=0)
    copies[4].wait()
    rows = rows_ref[...]
    high = rows.astype(BF16)
    mid, low = halves(rows - high.astype(F32))
    got = matmul(sel, high) + matmul(sel, mid) + matmul(sel, low)
    for z in range(groups):
        cols = slice(z * LANES, (z + 1) * LANES)
        for p in range(2):
            at = pl.ds(z * shards * PARTS + p, shards, stride=PARTS)
            out_ref[at, :] = got[p * shards : (p + 1) * shards, cols]


def side_kernel(counts_ref, upper_counts_ref, wide_ref, wide_upper_ref):
    for i in range(counts_ref.shape[0]):
        wide_ref[i * LANES : (i + 1) * LANES, :] = columns(counts_ref[i : i + 1, :])
    upper = upper_counts_ref[...]
    width = upper.shape[1]
    wide_upper_ref[...] = columns(jnp.concatenate([upper, jnp.zeros((1, LANES - width), F32)], axis=1))[:width]


def partial_sums(ids, parts_ref, out_ref):
    rows, members = out_ref.shape[0], parts_ref.shape[0]
    for at in range(0, rows, BLOCK):
        hot = onehot(ids - at == iota((BLOCK, members), 0))
        both = matmul(hot, parts_ref[...])
        out_ref[at : at + BLOCK, :] = both[:, :LANES] + both[:, LANES:]


def ids_of(oc_ref, sc_ref, core, width, places):
    owner = oc_ref[...]
    outer, inner, fold = places
    x = jnp.bitwise_and(lax.shift_right_logical(owner, 1), inner - 1)
    y = owner // (2 * inner)
    low, high = jnp.bitwise_and(y, fold - 1), y // fold
    first = x * outer + y
    other = low * (inner * outer // fold) + high * inner + x
    mine = jnp.bitwise_and(owner, 1)
    ids = jnp.where(mine == 1, first, other) * width + sc_ref[...]
    return jnp.where(mine == core, ids, -1)


def move_kernel(
    width, places, core_ref, got_ref, cent_ref, counts_ref, oc_ref, sc_ref,
    moved_hbm, new_counts_ref, send_ref, parts_ref, hits_ref, moved_ref, sem,
):
    sources = got_ref.shape[0] // PARTS
    lower = cent_ref.shape[0]
    part = [got_ref[pl.ds(i, sources, stride=PARTS), :] for i in range(PARTS)]
    meta = part[2]
    hits_ref[...] = jnp.sum(meta[:width], axis=0, keepdims=True)
    across = meta.T
    labels = jnp.concatenate([across[0:1, :], across[1:2, :]], axis=1).astype(jnp.int32)
    rows = jnp.concatenate(part[:2], axis=0)
    high, low = halves(rows)
    rhs = jnp.concatenate([high, low, jnp.ones((2 * sources, LANES), BF16)], axis=1)
    eye = iota((LANES, LANES), 0) == iota((LANES, LANES), 1)
    for i in range(lower // BLOCK):
        at = i * BLOCK
        hot = onehot(labels - at == iota((BLOCK, 2 * sources), 0))
        both = matmul(hot, rhs)
        summed = both[:, :LANES] + both[:, LANES : 2 * LANES]
        members = both[:, 2 * LANES :]
        old = cent_ref[at : at + BLOCK, :]
        total = counts_ref[at : at + BLOCK, :] + members
        moved = old + (summed - members * old) / total
        moved_ref[at : at + BLOCK, :] = moved
        high_m, low_m = halves(moved)
        parts_ref[at : at + BLOCK, :LANES] = high_m
        parts_ref[at : at + BLOCK, LANES:] = low_m
        for j in range(BLOCK // LANES):
            block = jnp.where(eye, total[j * LANES : (j + 1) * LANES], 0.0)
            row = i * (BLOCK // LANES) + j
            new_counts_ref[row : row + 1, :] = jnp.sum(block, axis=0, keepdims=True)
    copy = pltpu.make_async_copy(moved_ref, moved_hbm, sem)
    copy.start()
    partial_sums(ids_of(oc_ref, sc_ref, 1 - core_ref[0], width, places), parts_ref, send_ref)
    copy.wait()


def keep_kernel(
    width, places, core_ref, parts_ref, oc_ref, sc_ref, hits_ref, upper_counts_ref, keep_ref, members_ref, new_counts_ref,
):
    hits = hits_ref[...]
    members_ref[...] = columns(hits)[LANES - width :]
    new_counts_ref[...] = upper_counts_ref[...] + hits[:, LANES - width :]
    partial_sums(ids_of(oc_ref, sc_ref, core_ref[0], width, places), parts_ref, keep_ref)


def finish_kernel(pieces_ref, upper_ref, members_ref, counts_ref, out_ref):
    summed = jnp.sum(pieces_ref[...], axis=0)
    old, members = upper_ref[...], members_ref[...]
    out_ref[...] = old + (summed - members * old) / (counts_ref[...] + members)


VMEM = pl.BlockSpec(memory_space=pltpu.VMEM)
ANY = pl.BlockSpec(memory_space=pl.ANY)
SMEM = pl.BlockSpec(memory_space=pltpu.SMEM)


def call(kernel, ins, outs, flops, nbytes, name, out_specs=None, scratch=(), vmem=40):
    return pl.pallas_call(
        kernel,
        in_specs=ins,
        out_specs=out_specs or [VMEM] * len(outs),
        out_shape=[jax.ShapeDtypeStruct(s, d) for s, d in outs],
        scratch_shapes=list(scratch),
        compiler_params=pltpu.CompilerParams(vmem_limit_bytes=vmem * 1024 * 1024),
        cost_estimate=pl.CostEstimate(flops=flops, bytes_accessed=nbytes, transcendentals=0),
        name=name,
    )


def body(places, rows_data, owner_rows, slot_rows, centroids, counts, owner_cent, slot_cent, upper, upper_counts):
    groups, shards = lax.axis_size("rows"), lax.axis_size("plane")
    pairs = shards // 2
    devices = groups * shards
    batch, features = rows_data.shape
    lower = centroids.shape[0]
    width = upper.shape[0]
    core = jnp.bitwise_and(lax.axis_index("plane"), 1).astype(jnp.int32).reshape(1)
    oc = owner_cent.reshape(1, lower)
    sc = slot_cent.reshape(1, lower)
    half = width * pairs
    ints = lambda n: pltpu.VMEM((1, n), jnp.int32)
    (packed,) = call(
        functools.partial(pack_kernel, float(lower)),
        [ANY] * 5,
        [((devices * PARTS, LANES), F32)],
        10**8, 10**6, "pack", None,
        [pltpu.VMEM((batch, features), F32), ints(batch), ints(batch), ints(lower), ints(lower), pltpu.SemaphoreType.DMA((5,))],
        63,
    )(rows_data, owner_rows.reshape(1, batch), slot_rows.reshape(1, batch), oc, sc)
    got = lax.all_to_all(packed.reshape(devices, 1, PARTS * LANES), ("rows", "plane"), 0, 0, tiled=True)
    got = got.reshape(devices * PARTS, LANES)
    wide_counts, wide_upper = call(
        side_kernel,
        [VMEM] * 2,
        [((lower, LANES), F32), ((width, LANES), F32)],
        10**7, 10**6, "side",
    )(counts.reshape(lower // LANES, LANES), upper_counts.reshape(1, width))
    moved, new_counts, send, parts, hits = call(
        functools.partial(move_kernel, width, places),
        [SMEM] + [VMEM] * 5,
        [((lower, LANES), F32), ((lower // LANES, LANES), F32), ((half, LANES), F32), ((lower, 2 * LANES), BF16), ((1, LANES), F32)],
        4 * 10**9, 4 * 10**6, "move", [ANY] + [VMEM] * 4,
        [pltpu.VMEM((lower, LANES), F32), pltpu.SemaphoreType.DMA],
    )(core, got, centroids, wide_counts, oc, sc)
    arrived = lax.ppermute(send, "plane", [(s, s ^ 1) for s in range(shards)])
    keep, members, new_upper_counts = call(
        functools.partial(keep_kernel, width, places),
        [SMEM] + [VMEM] * 5,
        [((half, LANES), F32), ((width, LANES), F32), ((1, width), F32)],
        2 * 10**9, 2 * 10**6, "keep",
    )(core, parts, oc, sc, hits, upper_counts.reshape(1, width))
    outer, inner, fold = places
    at = lambda y, x, c: (y * inner + x) * 2 + c
    near = [[at(y, x, 1) for x in range(inner)] for y in range(outer)]
    near += [[at(h * fold + l, x, 0) for l in range(fold)] for h in range(outer // fold) for x in range(inner)]
    far = [[at(y, x, 1) for y in range(outer)] for x in range(inner)]
    far += [[at(h * fold + l, x, 0) for h in range(outer // fold) for x in range(inner)] for l in range(fold)]
    pair = (keep + arrived).reshape(inner, outer * width, LANES)
    merged = jnp.sum(lax.all_to_all(pair, "plane", 0, 0, axis_index_groups=near, tiled=True), axis=0)
    merged = merged.reshape(outer, width, LANES)
    pieces = lax.all_to_all(merged, "plane", 0, 0, axis_index_groups=far, tiled=True)
    (new_upper,) = call(
        finish_kernel,
        [VMEM] * 4,
        [((width, LANES), F32)],
        10**6, 10**6, "finish",
    )(pieces, upper, members, wide_upper)
    return moved, new_counts.reshape(lower), new_upper, new_upper_counts.reshape(width)


def solution(mesh):
    groups, outer, inner = mesh.devices.shape
    fine = Mesh(mesh.devices.reshape(groups, outer * inner), ("rows", "plane"))
    everyone = ("rows", "plane")
    inner = inner // 2
    return jax.shard_map(
        functools.partial(body, (outer, inner, inner)),
        mesh=fine,
        in_specs=(
            P(everyone, None), P(everyone, None), P(everyone),
            P("plane", "rows"), P("plane"), P("plane", None), P("plane"),
            P("plane", "rows"), P("plane"),
        ),
        out_specs=(P("plane", "rows"), P("plane"), P("plane", "rows"), P("plane")),
        check_vma=False,
    )
```

```python
import functools

import jax
import jax.numpy as jnp
from jax import lax
from jax.experimental import pallas as pl
from jax.experimental.pallas import tpu as pltpu
from jax.sharding import Mesh, PartitionSpec as P

F32 = jnp.float32
BF16 = jnp.bfloat16
LANES = 128
BLOCK = 256
PARTS = 3


def iota(shape, dim):
    return lax.broadcasted_iota(jnp.int32, shape, dim)


def onehot(mask):
    return jnp.where(mask, 1.0, 0.0).astype(BF16)


def matmul(a, b):
    return lax.dot_general(a, b, (((1,), (0,)), ((), ())), preferred_element_type=F32)


def halves(x):
    high = x.astype(BF16)
    return high, (x - high.astype(F32)).astype(BF16)


def columns(row):
    return jnp.broadcast_to(row, (LANES, LANES)).T


def pack_kernel(
    empty, rows_hbm, owner_hbm, slot_hbm, oc_hbm, sc_hbm, out_ref,
    rows_ref, owner_ref, slot_ref, oc_ref, sc_ref, sems,
):
    pairs = [
        (owner_hbm, owner_ref), (slot_hbm, slot_ref), (oc_hbm, oc_ref), (sc_hbm, sc_ref), (rows_hbm, rows_ref),
    ]
    copies = [pltpu.make_async_copy(src, dst, sems.at[i]) for i, (src, dst) in enumerate(pairs)]
    for copy in copies:
        copy.start()
    for copy in copies[:4]:
        copy.wait()
    batch, width = rows_ref.shape
    shards = batch
    groups = width // LANES
    lane = iota((shards, batch), 1)
    named = owner_ref[...] == iota((shards, batch), 0)
    first = jnp.min(jnp.where(named, lane.astype(F32), float(batch)), axis=1, keepdims=True)
    sel0 = lane.astype(F32) == first
    sel1 = jnp.logical_and(named, jnp.logical_not(sel0))
    slot = slot_ref[...].astype(F32)

    def label(sel):
        return jnp.sum(jnp.where(sel, slot - empty, 0.0), axis=1, keepdims=True) + empty

    members = oc_ref.shape[1]
    a = onehot(oc_ref[...] == iota((shards, members), 0))
    b = onehot(sc_ref[...] + (LANES - shards) == iota((LANES, members), 0))
    hits = lax.dot_general(a, b, (((1,), (1,)), ((), ())), preferred_element_type=F32)
    where = iota((shards, LANES), 1)
    meta = jnp.where(where == 0, label(sel0), jnp.where(where == 1, label(sel1), hits))
    for z in range(groups):
        out_ref[pl.ds(z * shards * PARTS + 2, shards, stride=PARTS), :] = meta
    sel = jnp.concatenate([onehot(sel0), onehot(sel1)], axis=0)
    copies[4].wait()
    rows = rows_ref[...]
    high = rows.astype(BF16)
    mid, low = halves(rows - high.astype(F32))
    got = matmul(sel, high) + matmul(sel, mid) + matmul(sel, low)
    for z in range(groups):
        cols = slice(z * LANES, (z + 1) * LANES)
        for p in range(2):
            at = pl.ds(z * shards * PARTS + p, shards, stride=PARTS)
            out_ref[at, :] = got[p * shards : (p + 1) * shards, cols]


def side_kernel(counts_ref, upper_counts_ref, wide_ref, wide_upper_ref):
    for i in range(counts_ref.shape[0]):
        wide_ref[i * LANES : (i + 1) * LANES, :] = columns(counts_ref[i : i + 1, :])
    upper = upper_counts_ref[...]
    width = upper.shape[1]
    wide_upper_ref[...] = columns(jnp.concatenate([upper, jnp.zeros((1, LANES - width), F32)], axis=1))[:width]


def partial_sums(ids, parts_ref, out_ref):
    rows, members = out_ref.shape[0], parts_ref.shape[0]
    for at in range(0, rows, BLOCK):
        hot = onehot(ids - at == iota((BLOCK, members), 0))
        both = matmul(hot, parts_ref[...])
        out_ref[at : at + BLOCK, :] = both[:, :LANES] + both[:, LANES:]


def ids_of(oc_ref, sc_ref, core, width, places):
    owner = oc_ref[...]
    outer, inner = places
    x = jnp.bitwise_and(lax.shift_right_logical(owner, 1), inner - 1)
    y = owner // (2 * inner)
    first = x * outer + y
    square = jnp.bitwise_and(y, 1) * 2 + jnp.bitwise_and(x, 1)
    other = square * (inner * outer // 4) + y // 2 * (inner // 2) + x // 2
    mine = jnp.bitwise_and(owner, 1)
    ids = jnp.where(mine == 1, first, other) * width + sc_ref[...]
    return jnp.where(mine == core, ids, -1)


def move_kernel(
    width, places, core_ref, got_ref, cent_ref, counts_ref, oc_ref, sc_ref,
    moved_hbm, new_counts_ref, send_ref, parts_ref, hits_ref, moved_ref, sem,
):
    sources = got_ref.shape[0] // PARTS
    lower = cent_ref.shape[0]
    part = [got_ref[pl.ds(i, sources, stride=PARTS), :] for i in range(PARTS)]
    meta = part[2]
    hits_ref[...] = jnp.sum(meta[:width], axis=0, keepdims=True)
    across = meta.T
    labels = jnp.concatenate([across[0:1, :], across[1:2, :]], axis=1).astype(jnp.int32)
    rows = jnp.concatenate(part[:2], axis=0)
    high, low = halves(rows)
    rhs = jnp.concatenate([high, low, jnp.ones((2 * sources, LANES), BF16)], axis=1)
    eye = iota((LANES, LANES), 0) == iota((LANES, LANES), 1)
    for i in range(lower // BLOCK):
        at = i * BLOCK
        hot = onehot(labels - at == iota((BLOCK, 2 * sources), 0))
        both = matmul(hot, rhs)
        summed = both[:, :LANES] + both[:, LANES : 2 * LANES]
        members = both[:, 2 * LANES :]
        old = cent_ref[at : at + BLOCK, :]
        total = counts_ref[at : at + BLOCK, :] + members
        moved = old + (summed - members * old) / total
        moved_ref[at : at + BLOCK, :] = moved
        high_m, low_m = halves(moved)
        parts_ref[at : at + BLOCK, :LANES] = high_m
        parts_ref[at : at + BLOCK, LANES:] = low_m
        for j in range(BLOCK // LANES):
            block = jnp.where(eye, total[j * LANES : (j + 1) * LANES], 0.0)
            row = i * (BLOCK // LANES) + j
            new_counts_ref[row : row + 1, :] = jnp.sum(block, axis=0, keepdims=True)
    copy = pltpu.make_async_copy(moved_ref, moved_hbm, sem)
    copy.start()
    partial_sums(ids_of(oc_ref, sc_ref, 1 - core_ref[0], width, places), parts_ref, send_ref)
    copy.wait()


def keep_kernel(
    width, places, core_ref, parts_ref, oc_ref, sc_ref, hits_ref, upper_counts_ref, keep_ref, members_ref, new_counts_ref,
):
    hits = hits_ref[...]
    members_ref[...] = columns(hits)[LANES - width :]
    new_counts_ref[...] = upper_counts_ref[...] + hits[:, LANES - width :]
    partial_sums(ids_of(oc_ref, sc_ref, core_ref[0], width, places), parts_ref, keep_ref)


def finish_kernel(pieces_ref, upper_ref, members_ref, counts_ref, out_ref):
    summed = jnp.sum(pieces_ref[...], axis=0)
    old, members = upper_ref[...], members_ref[...]
    out_ref[...] = old + (summed - members * old) / (counts_ref[...] + members)


VMEM = pl.BlockSpec(memory_space=pltpu.VMEM)
ANY = pl.BlockSpec(memory_space=pl.ANY)
SMEM = pl.BlockSpec(memory_space=pltpu.SMEM)


def call(kernel, ins, outs, flops, nbytes, name, out_specs=None, scratch=(), vmem=40):
    return pl.pallas_call(
        kernel,
        in_specs=ins,
        out_specs=out_specs or [VMEM] * len(outs),
        out_shape=[jax.ShapeDtypeStruct(s, d) for s, d in outs],
        scratch_shapes=list(scratch),
        compiler_params=pltpu.CompilerParams(vmem_limit_bytes=vmem * 1024 * 1024),
        cost_estimate=pl.CostEstimate(flops=flops, bytes_accessed=nbytes, transcendentals=0),
        name=name,
    )


def body(places, rows_data, owner_rows, slot_rows, centroids, counts, owner_cent, slot_cent, upper, upper_counts):
    groups, shards = lax.axis_size("rows"), lax.axis_size("plane")
    pairs = shards // 2
    devices = groups * shards
    batch, features = rows_data.shape
    lower = centroids.shape[0]
    width = upper.shape[0]
    core = jnp.bitwise_and(lax.axis_index("plane"), 1).astype(jnp.int32).reshape(1)
    oc = owner_cent.reshape(1, lower)
    sc = slot_cent.reshape(1, lower)
    half = width * pairs
    ints = lambda n: pltpu.VMEM((1, n), jnp.int32)
    (packed,) = call(
        functools.partial(pack_kernel, float(lower)),
        [ANY] * 5,
        [((devices * PARTS, LANES), F32)],
        10**8, 10**6, "pack", None,
        [pltpu.VMEM((batch, features), F32), ints(batch), ints(batch), ints(lower), ints(lower), pltpu.SemaphoreType.DMA((5,))],
        63,
    )(rows_data, owner_rows.reshape(1, batch), slot_rows.reshape(1, batch), oc, sc)
    got = lax.all_to_all(packed.reshape(devices, 1, PARTS * LANES), ("rows", "plane"), 0, 0, tiled=True)
    got = got.reshape(devices * PARTS, LANES)
    wide_counts, wide_upper = call(
        side_kernel,
        [VMEM] * 2,
        [((lower, LANES), F32), ((width, LANES), F32)],
        10**7, 10**6, "side",
    )(counts.reshape(lower // LANES, LANES), upper_counts.reshape(1, width))
    moved, new_counts, send, parts, hits = call(
        functools.partial(move_kernel, width, places),
        [SMEM] + [VMEM] * 5,
        [((lower, LANES), F32), ((lower // LANES, LANES), F32), ((half, LANES), F32), ((lower, 2 * LANES), BF16), ((1, LANES), F32)],
        4 * 10**9, 4 * 10**6, "move", [ANY] + [VMEM] * 4,
        [pltpu.VMEM((lower, LANES), F32), pltpu.SemaphoreType.DMA],
    )(core, got, centroids, wide_counts, oc, sc)
    arrived = lax.ppermute(send, "plane", [(s, s ^ 1) for s in range(shards)])
    keep, members, new_upper_counts = call(
        functools.partial(keep_kernel, width, places),
        [SMEM] + [VMEM] * 5,
        [((half, LANES), F32), ((width, LANES), F32), ((1, width), F32)],
        2 * 10**9, 2 * 10**6, "keep",
    )(core, parts, oc, sc, hits, upper_counts.reshape(1, width))
    outer, inner = places
    at = lambda y, x, c: (y * inner + x) * 2 + c
    corners = [(y, x) for y in range(2) for x in range(2)]
    squares = [(y, x) for y in range(0, outer, 2) for x in range(0, inner, 2)]
    near = [[at(y, x, 1) for x in range(inner)] for y in range(outer)]
    near += [[at(y + v, x + u, 0) for v, u in corners] for y, x in squares]
    far = [[at(y, x, 1) for y in range(outer)] for x in range(inner)]
    far += [[at(y + v, x + u, 0) for y, x in squares] for v, u in corners]
    pair = (keep + arrived).reshape(inner, outer * width, LANES)
    merged = jnp.sum(lax.all_to_all(pair, "plane", 0, 0, axis_index_groups=near, tiled=True), axis=0)
    merged = merged.reshape(outer, width, LANES)
    pieces = lax.all_to_all(merged, "plane", 0, 0, axis_index_groups=far, tiled=True)
    (new_upper,) = call(
        finish_kernel,
        [VMEM] * 4,
        [((width, LANES), F32)],
        10**6, 10**6, "finish",
    )(pieces, upper, members, wide_upper)
    return moved, new_counts.reshape(lower), new_upper, new_upper_counts.reshape(width)


def solution(mesh):
    groups, outer, inner = mesh.devices.shape
    fine = Mesh(mesh.devices.reshape(groups, outer * inner), ("rows", "plane"))
    everyone = ("rows", "plane")
    inner = inner // 2
    return jax.shard_map(
        functools.partial(body, (outer, inner)),
        mesh=fine,
        in_specs=(
            P(everyone, None), P(everyone, None), P(everyone),
            P("plane", "rows"), P("plane"), P("plane", None), P("plane"),
            P("plane", "rows"), P("plane"),
        ),
        out_specs=(P("plane", "rows"), P("plane"), P("plane", "rows"), P("plane")),
        check_vma=False,
    )
```

```python
import functools

import jax
import jax.numpy as jnp
from jax import lax
from jax.experimental import pallas as pl
from jax.experimental.pallas import tpu as pltpu
from jax.sharding import Mesh, PartitionSpec as P

F32 = jnp.float32
BF16 = jnp.bfloat16
LANES = 128
BLOCK = 256
PARTS = 3


def iota(shape, dim):
    return lax.broadcasted_iota(jnp.int32, shape, dim)


def onehot(mask):
    return jnp.where(mask, 1.0, 0.0).astype(BF16)


def matmul(a, b):
    return lax.dot_general(a, b, (((1,), (0,)), ((), ())), preferred_element_type=F32)


def halves(x):
    high = x.astype(BF16)
    return high, (x - high.astype(F32)).astype(BF16)


def columns(row):
    return jnp.broadcast_to(row, (LANES, LANES)).T


def pack_kernel(
    empty, rows_hbm, owner_hbm, slot_hbm, oc_hbm, sc_hbm, out_ref,
    rows_ref, owner_ref, slot_ref, oc_ref, sc_ref, sems,
):
    pairs = [
        (owner_hbm, owner_ref), (slot_hbm, slot_ref), (oc_hbm, oc_ref), (sc_hbm, sc_ref), (rows_hbm, rows_ref),
    ]
    copies = [pltpu.make_async_copy(src, dst, sems.at[i]) for i, (src, dst) in enumerate(pairs)]
    for copy in copies:
        copy.start()
    for copy in copies[:4]:
        copy.wait()
    batch, width = rows_ref.shape
    shards = batch
    groups = width // LANES
    lane = iota((shards, batch), 1)
    named = owner_ref[...] == iota((shards, batch), 0)
    first = jnp.min(jnp.where(named, lane.astype(F32), float(batch)), axis=1, keepdims=True)
    sel0 = lane.astype(F32) == first
    sel1 = jnp.logical_and(named, jnp.logical_not(sel0))
    slot = slot_ref[...].astype(F32)

    def label(sel):
        return jnp.sum(jnp.where(sel, slot - empty, 0.0), axis=1, keepdims=True) + empty

    members = oc_ref.shape[1]
    a = onehot(oc_ref[...] == iota((shards, members), 0))
    b = onehot(sc_ref[...] + (LANES - shards) == iota((LANES, members), 0))
    hits = lax.dot_general(a, b, (((1,), (1,)), ((), ())), preferred_element_type=F32)
    where = iota((shards, LANES), 1)
    meta = jnp.where(where == 0, label(sel0), jnp.where(where == 1, label(sel1), hits))
    for z in range(groups):
        out_ref[pl.ds(z * shards * PARTS + 2, shards, stride=PARTS), :] = meta
    sel = jnp.concatenate([onehot(sel0), onehot(sel1)], axis=0)
    copies[4].wait()
    rows = rows_ref[...]
    high = rows.astype(BF16)
    mid, low = halves(rows - high.astype(F32))
    got = matmul(sel, high) + matmul(sel, mid) + matmul(sel, low)
    for z in range(groups):
        cols = slice(z * LANES, (z + 1) * LANES)
        for p in range(2):
            at = pl.ds(z * shards * PARTS + p, shards, stride=PARTS)
            out_ref[at, :] = got[p * shards : (p + 1) * shards, cols]


def side_kernel(counts_ref, upper_counts_ref, wide_ref, wide_upper_ref):
    for i in range(counts_ref.shape[0]):
        wide_ref[i * LANES : (i + 1) * LANES, :] = columns(counts_ref[i : i + 1, :])
    upper = upper_counts_ref[...]
    width = upper.shape[1]
    wide_upper_ref[...] = columns(jnp.concatenate([upper, jnp.zeros((1, LANES - width), F32)], axis=1))[:width]


def partial_sums(ids, parts_ref, out_ref):
    rows, members = out_ref.shape[0], parts_ref.shape[0]
    for at in range(0, rows, BLOCK):
        hot = onehot(ids - at == iota((BLOCK, members), 0))
        both = matmul(hot, parts_ref[...])
        out_ref[at : at + BLOCK, :] = both[:, :LANES] + both[:, LANES:]


def ids_of(oc_ref, sc_ref, core, width, places):
    owner = oc_ref[...]
    outer, inner = places
    x = jnp.bitwise_and(lax.shift_right_logical(owner, 1), inner - 1)
    y = owner // (2 * inner)
    square = jnp.bitwise_and(y, 1) * 2 + jnp.bitwise_and(x, 1)
    place = square * (inner * outer // 4) + y // 2 * (inner // 2) + x // 2
    mine = jnp.bitwise_and(owner, 1)
    return jnp.where(mine == core, place * width + sc_ref[...], -1)


def move_kernel(
    width, places, core_ref, got_ref, cent_ref, counts_ref, oc_ref, sc_ref,
    moved_hbm, new_counts_ref, send_ref, parts_ref, hits_ref, moved_ref, sem,
):
    sources = got_ref.shape[0] // PARTS
    lower = cent_ref.shape[0]
    part = [got_ref[pl.ds(i, sources, stride=PARTS), :] for i in range(PARTS)]
    meta = part[2]
    hits_ref[...] = jnp.sum(meta[:width], axis=0, keepdims=True)
    across = meta.T
    labels = jnp.concatenate([across[0:1, :], across[1:2, :]], axis=1).astype(jnp.int32)
    rows = jnp.concatenate(part[:2], axis=0)
    high, low = halves(rows)
    rhs = jnp.concatenate([high, low, jnp.ones((2 * sources, LANES), BF16)], axis=1)
    eye = iota((LANES, LANES), 0) == iota((LANES, LANES), 1)
    for i in range(lower // BLOCK):
        at = i * BLOCK
        hot = onehot(labels - at == iota((BLOCK, 2 * sources), 0))
        both = matmul(hot, rhs)
        summed = both[:, :LANES] + both[:, LANES : 2 * LANES]
        members = both[:, 2 * LANES :]
        old = cent_ref[at : at + BLOCK, :]
        total = counts_ref[at : at + BLOCK, :] + members
        moved = old + (summed - members * old) / total
        moved_ref[at : at + BLOCK, :] = moved
        high_m, low_m = halves(moved)
        parts_ref[at : at + BLOCK, :LANES] = high_m
        parts_ref[at : at + BLOCK, LANES:] = low_m
        for j in range(BLOCK // LANES):
            block = jnp.where(eye, total[j * LANES : (j + 1) * LANES], 0.0)
            row = i * (BLOCK // LANES) + j
            new_counts_ref[row : row + 1, :] = jnp.sum(block, axis=0, keepdims=True)
    copy = pltpu.make_async_copy(moved_ref, moved_hbm, sem)
    copy.start()
    partial_sums(ids_of(oc_ref, sc_ref, 1 - core_ref[0], width, places), parts_ref, send_ref)
    copy.wait()


def keep_kernel(
    width, places, core_ref, parts_ref, oc_ref, sc_ref, hits_ref, upper_counts_ref, keep_ref, members_ref, new_counts_ref,
):
    hits = hits_ref[...]
    members_ref[...] = columns(hits)[LANES - width :]
    new_counts_ref[...] = upper_counts_ref[...] + hits[:, LANES - width :]
    partial_sums(ids_of(oc_ref, sc_ref, core_ref[0], width, places), parts_ref, keep_ref)


def finish_kernel(pieces_ref, upper_ref, members_ref, counts_ref, out_ref):
    summed = jnp.sum(pieces_ref[...], axis=0)
    old, members = upper_ref[...], members_ref[...]
    out_ref[...] = old + (summed - members * old) / (counts_ref[...] + members)


VMEM = pl.BlockSpec(memory_space=pltpu.VMEM)
ANY = pl.BlockSpec(memory_space=pl.ANY)
SMEM = pl.BlockSpec(memory_space=pltpu.SMEM)


def call(kernel, ins, outs, flops, nbytes, name, out_specs=None, scratch=(), vmem=40):
    return pl.pallas_call(
        kernel,
        in_specs=ins,
        out_specs=out_specs or [VMEM] * len(outs),
        out_shape=[jax.ShapeDtypeStruct(s, d) for s, d in outs],
        scratch_shapes=list(scratch),
        compiler_params=pltpu.CompilerParams(vmem_limit_bytes=vmem * 1024 * 1024),
        cost_estimate=pl.CostEstimate(flops=flops, bytes_accessed=nbytes, transcendentals=0),
        name=name,
    )


def body(places, rows_data, owner_rows, slot_rows, centroids, counts, owner_cent, slot_cent, upper, upper_counts):
    groups, shards = lax.axis_size("rows"), lax.axis_size("plane")
    pairs = shards // 2
    devices = groups * shards
    batch, features = rows_data.shape
    lower = centroids.shape[0]
    width = upper.shape[0]
    core = jnp.bitwise_and(lax.axis_index("plane"), 1).astype(jnp.int32).reshape(1)
    oc = owner_cent.reshape(1, lower)
    sc = slot_cent.reshape(1, lower)
    half = width * pairs
    ints = lambda n: pltpu.VMEM((1, n), jnp.int32)
    (packed,) = call(
        functools.partial(pack_kernel, float(lower)),
        [ANY] * 5,
        [((devices * PARTS, LANES), F32)],
        10**8, 10**6, "pack", None,
        [pltpu.VMEM((batch, features), F32), ints(batch), ints(batch), ints(lower), ints(lower), pltpu.SemaphoreType.DMA((5,))],
        63,
    )(rows_data, owner_rows.reshape(1, batch), slot_rows.reshape(1, batch), oc, sc)
    got = lax.all_to_all(packed.reshape(devices, 1, PARTS * LANES), ("rows", "plane"), 0, 0, tiled=True)
    got = got.reshape(devices * PARTS, LANES)
    wide_counts, wide_upper = call(
        side_kernel,
        [VMEM] * 2,
        [((lower, LANES), F32), ((width, LANES), F32)],
        10**7, 10**6, "side",
    )(counts.reshape(lower // LANES, LANES), upper_counts.reshape(1, width))
    moved, new_counts, send, parts, hits = call(
        functools.partial(move_kernel, width, places),
        [SMEM] + [VMEM] * 5,
        [((lower, LANES), F32), ((lower // LANES, LANES), F32), ((half, LANES), F32), ((lower, 2 * LANES), BF16), ((1, LANES), F32)],
        4 * 10**9, 4 * 10**6, "move", [ANY] + [VMEM] * 4,
        [pltpu.VMEM((lower, LANES), F32), pltpu.SemaphoreType.DMA],
    )(core, got, centroids, wide_counts, oc, sc)
    arrived = lax.ppermute(send, "plane", [(s, s ^ 1) for s in range(shards)])
    keep, members, new_upper_counts = call(
        functools.partial(keep_kernel, width, places),
        [SMEM] + [VMEM] * 5,
        [((half, LANES), F32), ((width, LANES), F32), ((1, width), F32)],
        2 * 10**9, 2 * 10**6, "keep",
    )(core, parts, oc, sc, hits, upper_counts.reshape(1, width))
    outer, inner = places
    at = lambda y, x, c: (y * inner + x) * 2 + c
    corners = [(y, x) for y in range(2) for x in range(2)]
    squares = [(y, x) for y in range(0, outer, 2) for x in range(0, inner, 2)]
    near = [[at(y + v, x + u, c) for v, u in corners] for y, x in squares for c in range(2)]
    far = [[at(y + v, x + u, c) for y, x in squares] for v, u in corners for c in range(2)]
    pair = (keep + arrived).reshape(inner, outer * width, LANES)
    merged = jnp.sum(lax.all_to_all(pair, "plane", 0, 0, axis_index_groups=near, tiled=True), axis=0)
    merged = merged.reshape(outer, width, LANES)
    pieces = lax.all_to_all(merged, "plane", 0, 0, axis_index_groups=far, tiled=True)
    (new_upper,) = call(
        finish_kernel,
        [VMEM] * 4,
        [((width, LANES), F32)],
        10**6, 10**6, "finish",
    )(pieces, upper, members, wide_upper)
    return moved, new_counts.reshape(lower), new_upper, new_upper_counts.reshape(width)


def solution(mesh):
    groups, outer, inner = mesh.devices.shape
    fine = Mesh(mesh.devices.reshape(groups, outer * inner), ("rows", "plane"))
    everyone = ("rows", "plane")
    inner = inner // 2
    return jax.shard_map(
        functools.partial(body, (outer, inner)),
        mesh=fine,
        in_specs=(
            P(everyone, None), P(everyone, None), P(everyone),
            P("plane", "rows"), P("plane"), P("plane", None), P("plane"),
            P("plane", "rows"), P("plane"),
        ),
        out_specs=(P("plane", "rows"), P("plane"), P("plane", "rows"), P("plane")),
        check_vma=False,
    )
```

```python
import functools

import jax
import jax.numpy as jnp
from jax import lax
from jax.experimental import pallas as pl
from jax.experimental.pallas import tpu as pltpu
from jax.sharding import Mesh, PartitionSpec as P

F32 = jnp.float32
BF16 = jnp.bfloat16
LANES = 128
BLOCK = 256
PARTS = 3


def iota(shape, dim):
    return lax.broadcasted_iota(jnp.int32, shape, dim)


def onehot(mask):
    return jnp.where(mask, 1.0, 0.0).astype(BF16)


def matmul(a, b):
    return lax.dot_general(a, b, (((1,), (0,)), ((), ())), preferred_element_type=F32)


def halves(x):
    high = x.astype(BF16)
    return high, (x - high.astype(F32)).astype(BF16)


def columns(row):
    return jnp.broadcast_to(row, (LANES, LANES)).T


def pack_kernel(
    empty, rows_hbm, owner_hbm, slot_hbm, oc_hbm, sc_hbm, out_ref,
    rows_ref, owner_ref, slot_ref, oc_ref, sc_ref, sems,
):
    moves = [
        (owner_hbm, owner_ref), (slot_hbm, slot_ref), (oc_hbm, oc_ref), (sc_hbm, sc_ref), (rows_hbm, rows_ref),
    ]
    copies = [pltpu.make_async_copy(src, dst, sems.at[i]) for i, (src, dst) in enumerate(moves)]
    for copy in copies:
        copy.start()
    for copy in copies[:4]:
        copy.wait()
    batch, width = rows_ref.shape
    shards = batch
    groups = width // LANES
    pairs = shards // 2

    def shard_at(shape):
        at = iota(shape, 0)
        return jnp.where(at < pairs, 2 * at, 2 * at - (shards - 1))

    lane = iota((shards, batch), 1)
    named = owner_ref[...] == shard_at((shards, batch))
    first = jnp.min(jnp.where(named, lane.astype(F32), float(batch)), axis=1, keepdims=True)
    sel0 = lane.astype(F32) == first
    sel1 = jnp.logical_and(named, jnp.logical_not(sel0))
    slot = slot_ref[...].astype(F32)

    def label(sel):
        return jnp.sum(jnp.where(sel, slot - empty, 0.0), axis=1, keepdims=True) + empty

    members = oc_ref.shape[1]
    a = onehot(oc_ref[...] == shard_at((shards, members)))
    b = onehot(sc_ref[...] + (LANES - shards) == iota((LANES, members), 0))
    hits = lax.dot_general(a, b, (((1,), (1,)), ((), ())), preferred_element_type=F32)
    where = iota((shards, LANES), 1)
    meta = jnp.where(where == 0, label(sel0), jnp.where(where == 1, label(sel1), hits))

    def spots(core, z, part):
        return pl.ds((core * groups + z) * pairs * PARTS + part, pairs, stride=PARTS)

    for z in range(groups):
        for core in range(2):
            out_ref[spots(core, z, 2), :] = meta[core * pairs : (core + 1) * pairs]
    sel = jnp.concatenate([onehot(sel0), onehot(sel1)], axis=0)
    copies[4].wait()
    rows = rows_ref[...]
    high = rows.astype(BF16)
    mid, low = halves(rows - high.astype(F32))
    got = matmul(sel, high) + matmul(sel, mid) + matmul(sel, low)
    for z in range(groups):
        cols = slice(z * LANES, (z + 1) * LANES)
        for p in range(2):
            for core in range(2):
                at = p * shards + core * pairs
                out_ref[spots(core, z, p), :] = got[at : at + pairs, cols]


def side_kernel(counts_ref, upper_counts_ref, wide_ref, wide_upper_ref):
    for i in range(counts_ref.shape[0]):
        wide_ref[i * LANES : (i + 1) * LANES, :] = columns(counts_ref[i : i + 1, :])
    upper = upper_counts_ref[...]
    width = upper.shape[1]
    wide_upper_ref[...] = columns(jnp.concatenate([upper, jnp.zeros((1, LANES - width), F32)], axis=1))[:width]


def partial_sums(ids, parts_ref, out_ref):
    rows, members = out_ref.shape[0], parts_ref.shape[0]
    for at in range(0, rows, BLOCK):
        hot = onehot(ids - at == iota((BLOCK, members), 0))
        both = matmul(hot, parts_ref[...])
        out_ref[at : at + BLOCK, :] = both[:, :LANES] + both[:, LANES:]


def ids_of(oc_ref, sc_ref, core, width, places):
    owner = oc_ref[...]
    outer, inner = places
    x = jnp.bitwise_and(lax.shift_right_logical(owner, 1), inner - 1)
    y = owner // (2 * inner)
    square = jnp.bitwise_and(y, 1) * 2 + jnp.bitwise_and(x, 1)
    place = square * (inner * outer // 4) + y // 2 * (inner // 2) + x // 2
    return jnp.where(jnp.bitwise_and(owner, 1) == core, place * width + sc_ref[...], -1)


def move_kernel(
    width, pairs, places, core_ref, got_ref, cent_ref, counts_ref, oc_ref, sc_ref,
    moved_hbm, new_counts_ref, send_ref, parts_ref, hits_ref, moved_ref, sem,
):
    sources = got_ref.shape[0] // PARTS
    lower = cent_ref.shape[0]
    part = [got_ref[pl.ds(i, sources, stride=PARTS), :] for i in range(PARTS)]
    meta = part[2]
    half = sources // 2
    counted = meta[:pairs] + meta[half : half + pairs]
    hits_ref[...] = jnp.sum(counted, axis=0, keepdims=True)
    across = meta.T
    labels = jnp.concatenate([across[0:1, :], across[1:2, :]], axis=1).astype(jnp.int32)
    rows = jnp.concatenate(part[:2], axis=0)
    high, low = halves(rows)
    rhs = jnp.concatenate([high, low, jnp.ones((2 * sources, LANES), BF16)], axis=1)
    eye = iota((LANES, LANES), 0) == iota((LANES, LANES), 1)
    for i in range(lower // BLOCK):
        at = i * BLOCK
        hot = onehot(labels - at == iota((BLOCK, 2 * sources), 0))
        both = matmul(hot, rhs)
        summed = both[:, :LANES] + both[:, LANES : 2 * LANES]
        members = both[:, 2 * LANES :]
        old = cent_ref[at : at + BLOCK, :]
        total = counts_ref[at : at + BLOCK, :] + members
        moved = old + (summed - members * old) / total
        moved_ref[at : at + BLOCK, :] = moved
        high_m, low_m = halves(moved)
        parts_ref[at : at + BLOCK, :LANES] = high_m
        parts_ref[at : at + BLOCK, LANES:] = low_m
        for j in range(BLOCK // LANES):
            block = jnp.where(eye, total[j * LANES : (j + 1) * LANES], 0.0)
            row = i * (BLOCK // LANES) + j
            new_counts_ref[row : row + 1, :] = jnp.sum(block, axis=0, keepdims=True)
    copy = pltpu.make_async_copy(moved_ref, moved_hbm, sem)
    copy.start()
    partial_sums(ids_of(oc_ref, sc_ref, 1 - core_ref[0], width, places), parts_ref, send_ref)
    copy.wait()


def keep_kernel(
    width, places, core_ref, parts_ref, oc_ref, sc_ref, hits_ref, upper_counts_ref, keep_ref, members_ref, new_counts_ref,
):
    hits = hits_ref[...]
    members_ref[...] = columns(hits)[LANES - width :]
    new_counts_ref[...] = upper_counts_ref[...] + hits[:, LANES - width :]
    partial_sums(ids_of(oc_ref, sc_ref, core_ref[0], width, places), parts_ref, keep_ref)


def finish_kernel(pieces_ref, upper_ref, members_ref, counts_ref, out_ref):
    summed = jnp.sum(pieces_ref[...], axis=0)
    old, members = upper_ref[...], members_ref[...]
    out_ref[...] = old + (summed - members * old) / (counts_ref[...] + members)


VMEM = pl.BlockSpec(memory_space=pltpu.VMEM)
ANY = pl.BlockSpec(memory_space=pl.ANY)
SMEM = pl.BlockSpec(memory_space=pltpu.SMEM)


def call(kernel, ins, outs, flops, nbytes, name, out_specs=None, scratch=(), vmem=40):
    return pl.pallas_call(
        kernel,
        in_specs=ins,
        out_specs=out_specs or [VMEM] * len(outs),
        out_shape=[jax.ShapeDtypeStruct(s, d) for s, d in outs],
        scratch_shapes=list(scratch),
        compiler_params=pltpu.CompilerParams(vmem_limit_bytes=vmem * 1024 * 1024),
        cost_estimate=pl.CostEstimate(flops=flops, bytes_accessed=nbytes, transcendentals=0),
        name=name,
    )


def body(rows_data, owner_rows, slot_rows, centroids, counts, owner_cent, slot_cent, upper, upper_counts):
    exchange = ("core", "rows", "yh", "yl", "xh", "xl")
    corner, square = ("yl", "xl"), ("yh", "xh")
    places = tuple(lax.axis_size(axes) for axes in (("yh", "yl"), ("xh", "xl")))
    groups = lax.axis_size("rows")
    shards = lax.axis_size(("yh", "yl", "xh", "xl", "core"))
    pairs = shards // 2
    devices = groups * shards
    batch, features = rows_data.shape
    lower = centroids.shape[0]
    width = upper.shape[0]
    core = lax.axis_index("core").astype(jnp.int32).reshape(1)
    oc = owner_cent.reshape(1, lower)
    sc = slot_cent.reshape(1, lower)
    half = width * pairs
    ints = lambda n: pltpu.VMEM((1, n), jnp.int32)
    (packed,) = call(
        functools.partial(pack_kernel, float(lower)),
        [ANY] * 5,
        [((devices * PARTS, LANES), F32)],
        10**8, 10**6, "pack", None,
        [pltpu.VMEM((batch, features), F32), ints(batch), ints(batch), ints(lower), ints(lower), pltpu.SemaphoreType.DMA((5,))],
        63,
    )(rows_data, owner_rows.reshape(1, batch), slot_rows.reshape(1, batch), oc, sc)
    got = lax.all_to_all(packed.reshape(devices, 1, PARTS * LANES), exchange, 0, 0, tiled=True)
    got = got.reshape(devices * PARTS, LANES)
    wide_counts, wide_upper = call(
        side_kernel,
        [VMEM] * 2,
        [((lower, LANES), F32), ((width, LANES), F32)],
        10**7, 10**6, "side",
    )(counts.reshape(lower // LANES, LANES), upper_counts.reshape(1, width))
    moved, new_counts, send, parts, hits = call(
        functools.partial(move_kernel, width, pairs, places),
        [SMEM] + [VMEM] * 5,
        [((lower, LANES), F32), ((lower // LANES, LANES), F32), ((half, LANES), F32), ((lower, 2 * LANES), BF16), ((1, LANES), F32)],
        4 * 10**9, 4 * 10**6, "move", [ANY] + [VMEM] * 4,
        [pltpu.VMEM((lower, LANES), F32), pltpu.SemaphoreType.DMA],
    )(core, got, centroids, wide_counts, oc, sc)
    arrived = lax.ppermute(send, "core", [(0, 1), (1, 0)])
    keep, members, new_upper_counts = call(
        functools.partial(keep_kernel, width, places),
        [SMEM] + [VMEM] * 5,
        [((half, LANES), F32), ((width, LANES), F32), ((1, width), F32)],
        2 * 10**9, 2 * 10**6, "keep",
    )(core, parts, oc, sc, hits, upper_counts.reshape(1, width))
    pair = (keep + arrived).reshape(4, half // 4, LANES)
    merged = jnp.sum(lax.all_to_all(pair, corner, 0, 0, tiled=True), axis=0)
    pieces = lax.all_to_all(merged.reshape(pairs // 4, width, LANES), square, 0, 0, tiled=True)
    (new_upper,) = call(
        finish_kernel,
        [VMEM] * 4,
        [((width, LANES), F32)],
        10**6, 10**6, "finish",
    )(pieces, upper, members, wide_upper)
    return moved, new_counts.reshape(lower), new_upper, new_upper_counts.reshape(width)


def solution(mesh):
    groups, outer, inner = mesh.devices.shape
    shape = (groups, outer // 2, 2, inner // 4, 2, 2)
    fine = Mesh(mesh.devices.reshape(shape), ("rows", "yh", "yl", "xh", "xl", "core"))
    plane = ("yh", "yl", "xh", "xl", "core")
    everyone = ("rows", *plane)
    return jax.shard_map(
        body,
        mesh=fine,
        in_specs=(
            P(everyone, None), P(everyone, None), P(everyone),
            P(plane, "rows"), P(plane), P(plane, None), P(plane),
            P(plane, "rows"), P(plane),
        ),
        out_specs=(P(plane, "rows"), P(plane), P(plane, "rows"), P(plane)),
        check_vma=False,
    )
```

```python
import functools

import jax
import jax.numpy as jnp
from jax import lax
from jax.experimental import pallas as pl
from jax.experimental.pallas import tpu as pltpu
from jax.sharding import Mesh, PartitionSpec as P

F32 = jnp.float32
BF16 = jnp.bfloat16
LANES = 128
BLOCK = 256
PARTS = 3


def iota(shape, dim):
    return lax.broadcasted_iota(jnp.int32, shape, dim)


def onehot(mask):
    return jnp.where(mask, 1.0, 0.0).astype(BF16)


def matmul(a, b):
    return lax.dot_general(a, b, (((1,), (0,)), ((), ())), preferred_element_type=F32)


def halves(x):
    high = x.astype(BF16)
    return high, (x - high.astype(F32)).astype(BF16)


def columns(row):
    return jnp.broadcast_to(row, (LANES, LANES)).T


def pack_kernel(
    empty, rows_hbm, owner_hbm, slot_hbm, oc_hbm, sc_hbm, out_ref,
    rows_ref, owner_ref, slot_ref, oc_ref, sc_ref, sems,
):
    moves = [
        (owner_hbm, owner_ref), (slot_hbm, slot_ref), (oc_hbm, oc_ref), (sc_hbm, sc_ref), (rows_hbm, rows_ref),
    ]
    copies = [pltpu.make_async_copy(src, dst, sems.at[i]) for i, (src, dst) in enumerate(moves)]
    for copy in copies:
        copy.start()
    for copy in copies[:4]:
        copy.wait()
    batch, width = rows_ref.shape
    shards = batch
    groups = width // LANES
    pairs = shards // 2

    def shard_at(shape):
        at = iota(shape, 0)
        return jnp.where(at < pairs, 2 * at, 2 * at - (shards - 1))

    lane = iota((shards, batch), 1)
    named = owner_ref[...] == shard_at((shards, batch))
    first = jnp.min(jnp.where(named, lane.astype(F32), float(batch)), axis=1, keepdims=True)
    sel0 = lane.astype(F32) == first
    sel1 = jnp.logical_and(named, jnp.logical_not(sel0))
    slot = slot_ref[...].astype(F32)

    def label(sel):
        return jnp.sum(jnp.where(sel, slot - empty, 0.0), axis=1, keepdims=True) + empty

    members = oc_ref.shape[1]
    a = onehot(oc_ref[...] == shard_at((shards, members)))
    b = onehot(sc_ref[...] + (LANES - shards) == iota((LANES, members), 0))
    hits = lax.dot_general(a, b, (((1,), (1,)), ((), ())), preferred_element_type=F32)
    where = iota((shards, LANES), 1)
    meta = jnp.where(where == 0, label(sel0), jnp.where(where == 1, label(sel1), hits))

    def spots(core, z, part):
        return pl.ds((core * groups + z) * pairs * PARTS + part, pairs, stride=PARTS)

    for z in range(groups):
        for core in range(2):
            out_ref[spots(core, z, 2), :] = meta[core * pairs : (core + 1) * pairs]
    sel = jnp.concatenate([onehot(sel0), onehot(sel1)], axis=0)
    copies[4].wait()
    rows = rows_ref[...]
    high = rows.astype(BF16)
    mid, low = halves(rows - high.astype(F32))
    got = matmul(sel, high) + matmul(sel, mid) + matmul(sel, low)
    for z in range(groups):
        cols = slice(z * LANES, (z + 1) * LANES)
        for p in range(2):
            for core in range(2):
                at = p * shards + core * pairs
                out_ref[spots(core, z, p), :] = got[at : at + pairs, cols]


def side_kernel(counts_ref, upper_counts_ref, wide_ref, wide_upper_ref):
    for i in range(counts_ref.shape[0]):
        wide_ref[i * LANES : (i + 1) * LANES, :] = columns(counts_ref[i : i + 1, :])
    upper = upper_counts_ref[...]
    width = upper.shape[1]
    wide_upper_ref[...] = columns(jnp.concatenate([upper, jnp.zeros((1, LANES - width), F32)], axis=1))[:width]


def partial_sums(ids, parts_ref, out_ref):
    rows, members = out_ref.shape[0], parts_ref.shape[0]
    for at in range(0, rows, BLOCK):
        hot = onehot(ids - at == iota((BLOCK, members), 0))
        both = matmul(hot, parts_ref[...])
        out_ref[at : at + BLOCK, :] = both[:, :LANES] + both[:, LANES:]


def ids_of(oc_ref, sc_ref, core, width, places):
    owner = oc_ref[...]
    outer, inner = places
    x = jnp.bitwise_and(lax.shift_right_logical(owner, 1), inner - 1)
    y = owner // (2 * inner)
    square = jnp.bitwise_and(x, 1) * 2 + jnp.bitwise_and(y, 1)
    place = square * (inner * outer // 4) + x // 2 * (outer // 2) + y // 2
    return jnp.where(jnp.bitwise_and(owner, 1) == core, place * width + sc_ref[...], -1)


def move_kernel(
    width, pairs, places, core_ref, got_ref, cent_ref, counts_ref, oc_ref, sc_ref,
    moved_hbm, new_counts_ref, send_ref, parts_ref, hits_ref, moved_ref, sem,
):
    sources = got_ref.shape[0] // PARTS
    lower = cent_ref.shape[0]
    part = [got_ref[pl.ds(i, sources, stride=PARTS), :] for i in range(PARTS)]
    meta = part[2]
    half = sources // 2
    counted = meta[:pairs] + meta[half : half + pairs]
    hits_ref[...] = jnp.sum(counted, axis=0, keepdims=True)
    across = meta.T
    labels = jnp.concatenate([across[0:1, :], across[1:2, :]], axis=1).astype(jnp.int32)
    rows = jnp.concatenate(part[:2], axis=0)
    high, low = halves(rows)
    rhs = jnp.concatenate([high, low, jnp.ones((2 * sources, LANES), BF16)], axis=1)
    eye = iota((LANES, LANES), 0) == iota((LANES, LANES), 1)
    for i in range(lower // BLOCK):
        at = i * BLOCK
        hot = onehot(labels - at == iota((BLOCK, 2 * sources), 0))
        both = matmul(hot, rhs)
        summed = both[:, :LANES] + both[:, LANES : 2 * LANES]
        members = both[:, 2 * LANES :]
        old = cent_ref[at : at + BLOCK, :]
        total = counts_ref[at : at + BLOCK, :] + members
        moved = old + (summed - members * old) / total
        moved_ref[at : at + BLOCK, :] = moved
        high_m, low_m = halves(moved)
        parts_ref[at : at + BLOCK, :LANES] = high_m
        parts_ref[at : at + BLOCK, LANES:] = low_m
        for j in range(BLOCK // LANES):
            block = jnp.where(eye, total[j * LANES : (j + 1) * LANES], 0.0)
            row = i * (BLOCK // LANES) + j
            new_counts_ref[row : row + 1, :] = jnp.sum(block, axis=0, keepdims=True)
    copy = pltpu.make_async_copy(moved_ref, moved_hbm, sem)
    copy.start()
    partial_sums(ids_of(oc_ref, sc_ref, 1 - core_ref[0], width, places), parts_ref, send_ref)
    copy.wait()


def keep_kernel(
    width, places, core_ref, parts_ref, oc_ref, sc_ref, hits_ref, upper_counts_ref, keep_ref, members_ref, new_counts_ref,
):
    hits = hits_ref[...]
    members_ref[...] = columns(hits)[LANES - width :]
    new_counts_ref[...] = upper_counts_ref[...] + hits[:, LANES - width :]
    partial_sums(ids_of(oc_ref, sc_ref, core_ref[0], width, places), parts_ref, keep_ref)


def finish_kernel(pieces_ref, upper_ref, members_ref, counts_ref, out_ref):
    summed = jnp.sum(pieces_ref[...], axis=0)
    old, members = upper_ref[...], members_ref[...]
    out_ref[...] = old + (summed - members * old) / (counts_ref[...] + members)


VMEM = pl.BlockSpec(memory_space=pltpu.VMEM)
ANY = pl.BlockSpec(memory_space=pl.ANY)
SMEM = pl.BlockSpec(memory_space=pltpu.SMEM)


def call(kernel, ins, outs, flops, nbytes, name, out_specs=None, scratch=(), vmem=40):
    return pl.pallas_call(
        kernel,
        in_specs=ins,
        out_specs=out_specs or [VMEM] * len(outs),
        out_shape=[jax.ShapeDtypeStruct(s, d) for s, d in outs],
        scratch_shapes=list(scratch),
        compiler_params=pltpu.CompilerParams(vmem_limit_bytes=vmem * 1024 * 1024),
        cost_estimate=pl.CostEstimate(flops=flops, bytes_accessed=nbytes, transcendentals=0),
        name=name,
    )


def body(rows_data, owner_rows, slot_rows, centroids, counts, owner_cent, slot_cent, upper, upper_counts):
    exchange = ("core", "rows", "yh", "yl", "xh", "xl")
    corner, square = ("xl", "yl"), ("xh", "yh")
    places = tuple(lax.axis_size(axes) for axes in (("yh", "yl"), ("xh", "xl")))
    groups = lax.axis_size("rows")
    shards = lax.axis_size(("yh", "yl", "xh", "xl", "core"))
    pairs = shards // 2
    devices = groups * shards
    batch, features = rows_data.shape
    lower = centroids.shape[0]
    width = upper.shape[0]
    core = lax.axis_index("core").astype(jnp.int32).reshape(1)
    oc = owner_cent.reshape(1, lower)
    sc = slot_cent.reshape(1, lower)
    half = width * pairs
    ints = lambda n: pltpu.VMEM((1, n), jnp.int32)
    (packed,) = call(
        functools.partial(pack_kernel, float(lower)),
        [ANY] * 5,
        [((devices * PARTS, LANES), F32)],
        10**8, 10**6, "pack", None,
        [pltpu.VMEM((batch, features), F32), ints(batch), ints(batch), ints(lower), ints(lower), pltpu.SemaphoreType.DMA((5,))],
        63,
    )(rows_data, owner_rows.reshape(1, batch), slot_rows.reshape(1, batch), oc, sc)
    got = lax.all_to_all(packed.reshape(devices, 1, PARTS * LANES), exchange, 0, 0, tiled=True)
    got = got.reshape(devices * PARTS, LANES)
    wide_counts, wide_upper = call(
        side_kernel,
        [VMEM] * 2,
        [((lower, LANES), F32), ((width, LANES), F32)],
        10**7, 10**6, "side",
    )(counts.reshape(lower // LANES, LANES), upper_counts.reshape(1, width))
    moved, new_counts, send, parts, hits = call(
        functools.partial(move_kernel, width, pairs, places),
        [SMEM] + [VMEM] * 5,
        [((lower, LANES), F32), ((lower // LANES, LANES), F32), ((half, LANES), F32), ((lower, 2 * LANES), BF16), ((1, LANES), F32)],
        4 * 10**9, 4 * 10**6, "move", [ANY] + [VMEM] * 4,
        [pltpu.VMEM((lower, LANES), F32), pltpu.SemaphoreType.DMA],
    )(core, got, centroids, wide_counts, oc, sc)
    arrived = lax.ppermute(send, "core", [(0, 1), (1, 0)])
    keep, members, new_upper_counts = call(
        functools.partial(keep_kernel, width, places),
        [SMEM] + [VMEM] * 5,
        [((half, LANES), F32), ((width, LANES), F32), ((1, width), F32)],
        2 * 10**9, 2 * 10**6, "keep",
    )(core, parts, oc, sc, hits, upper_counts.reshape(1, width))
    pair = (keep + arrived).reshape(4, half // 4, LANES)
    merged = jnp.sum(lax.all_to_all(pair, corner, 0, 0, tiled=True), axis=0)
    pieces = lax.all_to_all(merged.reshape(pairs // 4, width, LANES), square, 0, 0, tiled=True)
    (new_upper,) = call(
        finish_kernel,
        [VMEM] * 4,
        [((width, LANES), F32)],
        10**6, 10**6, "finish",
    )(pieces, upper, members, wide_upper)
    return moved, new_counts.reshape(lower), new_upper, new_upper_counts.reshape(width)


def solution(mesh):
    groups, outer, inner = mesh.devices.shape
    shape = (groups, outer // 2, 2, inner // 4, 2, 2)
    fine = Mesh(mesh.devices.reshape(shape), ("rows", "yh", "yl", "xh", "xl", "core"))
    plane = ("yh", "yl", "xh", "xl", "core")
    everyone = ("rows", *plane)
    return jax.shard_map(
        body,
        mesh=fine,
        in_specs=(
            P(everyone, None), P(everyone, None), P(everyone),
            P(plane, "rows"), P(plane), P(plane, None), P(plane),
            P(plane, "rows"), P(plane),
        ),
        out_specs=(P(plane, "rows"), P(plane), P(plane, "rows"), P(plane)),
        check_vma=False,
    )
```
